32 devices in a mesh: frames: 8 (over y, x, core), expert: 4 (over z).
Axes of the slice: x: 2, y: 2, z: 4, core: 2. Of those that a mesh axis runs over, the one named last changes fastest.
Arguments:
- residual: bfloat16 [8, 512, 1152], P('frames', 'expert'), may hold values from -6 to 6
- queries: bfloat16 [8, 512, 1152], P('frames', 'expert'), may hold values from -8 to 8
- keys_in: bfloat16 [8, 512, 1152], P('frames', 'expert'), may hold values from -8 to 8
- values: bfloat16 [8, 512, 1152], P('frames', 'expert'), may hold values from -6 to 6
- w_out: bfloat16 [1152, 1152], replicated, may hold values from -0.1875 to 0.1875
- norm_gain: float32 [1152], replicated, may hold values from 0.5 to 2
- w_router: bfloat16 [1152, 16], replicated, may hold values from -0.1875 to 0.1875
- routes: int32 [4, 8, 128, 2], P('expert', 'frames'), may hold values from 0 to 15, all different within a row; in each aligned block of 128 rows (0 to 127, 128 to 255, ..., all dimensions but the last counted through in order) at most 32 rows name the same one
- w_gate: bfloat16 [32, 1152, 512], P(('frames', 'expert')), may hold values from -0.1875 to 0.1875
- w_up: bfloat16 [32, 1152, 512], P(('frames', 'expert')), may hold values from -0.1875 to 0.1875
- w_down: bfloat16 [32, 512, 1152], P(('frames', 'expert')), may hold values from -0.1875 to 0.1875
- d_out: bfloat16 [8, 512, 1152], P('frames', 'expert'), may hold values from -2 to 2
Outputs:
- block_out: bfloat16 [8, 512, 1152], P('frames', 'expert')
- d_hidden: bfloat16 [8, 512, 1152], P('frames', 'expert')
- d_gate: float32 [32, 1152, 512], P(('frames', 'expert'))
- d_up: float32 [32, 1152, 512], P(('frames', 'expert'))
- d_down: float32 [32, 512, 1152], P(('frames', 'expert'))
The draws below stay inside these ranges and needn't reach their ends.
Inputs may be any that keep to these rules, and one draw needn't show every extreme that they name: `routes`: the two experts of a token differ. In the rows of one device (the aligned blocks of 128 rows over the flattened leading dimensions) no expert is named more than 32 times; some expert is named exactly 32 times in some of these blocks.
All inputs are finite; a program needn't handle non-finite values.
Results may differ from the reference program's by a relative error of at most 0.018.
Values may be sent and summed in bfloat16 or wider, within the bound.
A program may use at most 128 MiB of HBM per device.

```python
import math
import jax
import jax.numpy as jnp
import numpy as np
from jax import lax

D = 1152
H = 16
FF = 1024
P_SIZE = 512
FFH = 512
F = 8
GROUPS = 4
PQ = 128
TOK_DEV = 128
EXPERTS = 16
CAP = 32
DEVICES = 32


def attention_pair(key):
    base = jax.random.fold_in(key, 11)
    streams = jax.random.split(base, 2)
    queries = jnp.clip(jax.random.normal(streams[0], (F, P_SIZE, D), jnp.float32), -8.0, 8.0)
    keys_out = jnp.clip(jax.random.normal(streams[1], (F, P_SIZE, D), jnp.float32), -8.0, 8.0)
    return (queries, keys_out)


def draw_queries(key, part):
    return attention_pair(key)[0].astype(jnp.bfloat16)


def draw_keys_in(key, part):
    return attention_pair(key)[1].astype(jnp.bfloat16)


def block_scale(own_key, shape, cuts, least, largest):
    factor_of, own = 1.0, jax.random.fold_in(own_key, 6)
    for axis_at, parts in cuts:
        steps = jnp.exp(jax.random.uniform(jax.random.fold_in(own, axis_at), (parts,), jnp.float32, least / len(cuts), largest / len(cuts)))
        factor_of = factor_of * jnp.repeat(steps, shape[axis_at] // parts).reshape([-1 if axis == axis_at else 1 for axis in range(len(shape))])
    return factor_of


def assign_block(rng, own, number, rows, count, top, limit, slope):
    sequence = jax.random.permutation(rng, count)
    crowded, common = load_shares(count, rows * top, limit, slope, True), load_shares(count, rows * top, limit, slope, False)
    places = jnp.arange(count)

    def named(tallies, turn):
        used = int((tallies > 0).sum())
        fixed = max(1, used // 4)
        passed = fixed + (places - fixed + turn * (used - fixed)) % max(1, count - fixed)
        return jnp.zeros((count,), jnp.int32).at[sequence[jnp.where(places < fixed, places, passed)]].set(jnp.asarray(tallies, jnp.int32))

    tallies = jnp.where(number % 4 == 0, named(crowded, number // 4), named(common, number - number // 4 - 1))
    mixed = jax.random.permutation(jax.random.fold_in(own, 3), count)
    source_of, sink = mixed[0:count // 2 * 2:2], mixed[1:count // 2 * 2:2]
    slack = jnp.minimum(tallies[source_of] - 1, limit - tallies[sink]) // 2
    slack = jnp.where((source_of == sequence[0]) | (sink == sequence[0]) | (tallies[sink] == 0), 0, jnp.maximum(slack, 0))
    passed = jax.random.randint(jax.random.fold_in(own, 4), (count // 2,), 0, 1 << 20) % (slack + 1)
    tallies = tallies.at[source_of].add(-passed).at[sink].add(passed)
    members = jnp.searchsorted(jnp.cumsum(tallies), jnp.arange(rows * top), side="right").astype(jnp.int32)
    table = members.reshape(top, rows).T
    table = table[jax.random.permutation(jax.random.fold_in(own, 1), rows)]
    turn = jax.random.randint(jax.random.fold_in(own, 2), (rows, 1), 0, top)
    return jnp.take_along_axis(table, (jnp.arange(top)[None, :] + turn) % top, axis=1)


def load_shares(count, total, limit, slope, full):
    portions = [(1 << 20) // math.isqrt(rank ** slope) + 1 for rank in range(1, count + 1)]
    largest = limit if full else min(limit, max(-(-total // count), total * portions[0] // sum(portions)))
    least = 1 if total - largest >= count - 1 else 0
    holding, spare = [largest] + [least] * (count - 1), total - largest - least * (count - 1)
    while spare > 0:
        movable = [i for i in range(1, count) if holding[i] < largest] or [i for i in range(1, count) if holding[i] < limit]
        whole, remaining = sum([portions[i] for i in movable]), spare
        for i in movable:
            more = min(limit - holding[i], max(1, remaining * portions[i] // whole), spare)
            holding[i] = holding[i] + more
            spare = spare - more
    return np.array(holding)


def gaussian(own_key, extent, deviation, limit, shards=(), kind=jnp.bfloat16):
    entries = deviation * jax.random.normal(own_key, extent, jnp.float32)
    if shards:
        entries = entries * block_scale(own_key, extent, shards, -0.22, 0.18)
    return jnp.clip(entries, -limit, limit).astype(kind)


def setup_inputs(seed: int = 0) -> dict:
    keys = jax.random.split(jax.random.key(seed), 13)
    residual = gaussian(keys[0], (F, P_SIZE, D), 1.0, 6.0, ((0, 8), (1, 4)))
    queries = draw_queries(jax.random.fold_in(keys[12], 71), 0)
    keys_in = draw_keys_in(jax.random.fold_in(keys[12], 71), 0)
    values = gaussian(keys[3], (F, P_SIZE, D), 1.0, 6.0, ((0, 8), (1, 4)))
    w_out = gaussian(keys[4], (D, D), D ** -0.5, 0.1875)
    norm_gain = jnp.clip(jnp.exp(jax.random.uniform(keys[5], (D,), jnp.float32, math.log(0.5), math.log(2.0))), 0.5, 2.0)
    w_router = gaussian(keys[6], (D, EXPERTS), D ** -0.5, 0.1875)
    routes_keys = jax.random.split(jax.random.fold_in(keys[7], 1), GROUPS * F * PQ // TOK_DEV)
    routes_turns = jax.random.permutation(jax.random.fold_in(keys[7], 3), GROUPS * F * PQ // TOK_DEV)
    routes = jax.vmap(lambda own, number: assign_block(jax.random.fold_in(keys[7], 2), own, number, TOK_DEV, EXPERTS, 2, CAP, 2))(routes_keys, routes_turns).reshape((GROUPS, F, PQ, 2))
    w_gate = gaussian(keys[8], (2 * EXPERTS, D, FFH), D ** -0.5, 0.1875, ((0, 32),))
    w_up = gaussian(keys[9], (2 * EXPERTS, D, FFH), D ** -0.5, 0.1875, ((0, 32),))
    w_down = gaussian(keys[10], (2 * EXPERTS, FFH, D), FF ** -0.5, 0.1875, ((0, 32),))
    d_out = gaussian(keys[11], (F, P_SIZE, D), 0.25, 2.0, ((0, 8), (1, 4)))
    return {"residual": residual, "queries": queries, "keys_in": keys_in, "values": values, "w_out": w_out, "norm_gain": norm_gain, "w_router": w_router, "routes": routes, "w_gate": w_gate, "w_up": w_up, "w_down": w_down, "d_out": d_out}


def expert_pass(normed_rows, scaled_rows):

    def run(operands):
        rows, gate_pair, up_pair, down_pair = operands
        inputs_in = normed_rows[rows]
        grad_in = scaled_rows[rows]
        expert_sum = jnp.zeros((rows.shape[0], inputs_in.shape[1]), jnp.float32)
        input_sum = jnp.zeros((rows.shape[0], inputs_in.shape[1]), jnp.float32)
        gate_grads = []
        up_grads = []
        down_grads = []
        for half_idx in range(2):
            gate_w = gate_pair[half_idx]
            up_w = up_pair[half_idx]
            down_w = down_pair[half_idx]
            pre_gate = jnp.dot(inputs_in, gate_w, preferred_element_type=jnp.float32)
            pre_up = jnp.dot(inputs_in, up_w, preferred_element_type=jnp.float32)
            gate_sig = jax.nn.sigmoid(pre_gate)
            gate_act = pre_gate * gate_sig
            hidden_units = (gate_act * pre_up).astype(jnp.bfloat16)
            part_out = jnp.dot(hidden_units, down_w, preferred_element_type=jnp.float32).astype(jnp.bfloat16)
            expert_sum = expert_sum + lax.optimization_barrier(part_out).astype(jnp.float32)
            d_units = jnp.dot(grad_in, down_w.T, preferred_element_type=jnp.float32)
            d_pre_gate = (d_units * pre_up * (gate_sig + pre_gate * gate_sig * (1.0 - gate_sig))).astype(jnp.bfloat16)
            d_pre_up = (d_units * gate_act).astype(jnp.bfloat16)
            down_grads.append(jnp.dot(hidden_units.T, grad_in, preferred_element_type=jnp.float32))
            gate_grads.append(jnp.dot(inputs_in.T, d_pre_gate, preferred_element_type=jnp.float32))
            up_grads.append(jnp.dot(inputs_in.T, d_pre_up, preferred_element_type=jnp.float32))
            part_in = (jnp.dot(d_pre_gate, gate_w.T, preferred_element_type=jnp.float32) + jnp.dot(d_pre_up, up_w.T, preferred_element_type=jnp.float32)).astype(jnp.bfloat16)
            input_sum = input_sum + lax.optimization_barrier(part_in).astype(jnp.float32)
        expert_sum = lax.optimization_barrier(expert_sum.astype(jnp.bfloat16)).astype(jnp.float32)
        input_sum = lax.optimization_barrier(input_sum.astype(jnp.bfloat16)).astype(jnp.float32)
        return (expert_sum, input_sum, jnp.stack(gate_grads), jnp.stack(up_grads), jnp.stack(down_grads))
    return run

def reference(residual, queries, keys_in, values, w_out, norm_gain, w_router, routes, w_gate, w_up, w_down, d_out):
    head_width = D // H

    def heads_view(tensor):
        return tensor.astype(jnp.float32).reshape(F, P_SIZE, H, head_width)
    scores = jnp.einsum('fphd,gphd->phfg', heads_view(queries), heads_view(keys_in), precision=lax.Precision.HIGHEST) * head_width ** (-0.5)
    row_peak = lax.optimization_barrier(jnp.max(scores, axis=-1, keepdims=True))
    weights = jnp.exp(scores - row_peak)
    attn_probs = (weights / lax.optimization_barrier(jnp.sum(weights, axis=-1, keepdims=True))).astype(jnp.bfloat16)
    attended = jnp.einsum('phfg,gphd->fphd', attn_probs.astype(jnp.float32), heads_view(values), precision=lax.Precision.HIGHEST).astype(jnp.bfloat16)
    tok_total = F * P_SIZE
    attended = attended.reshape(tok_total, D)
    stream = residual.reshape(tok_total, D).astype(jnp.float32) + jnp.dot(attended, w_out, preferred_element_type=jnp.float32)
    hidden = stream.astype(jnp.bfloat16)
    hidden_float = hidden.astype(jnp.float32)
    inv_rms = lax.rsqrt(lax.optimization_barrier(jnp.mean(hidden_float * hidden_float, axis=-1, keepdims=True)) + 1e-06)
    normed = (hidden_float * inv_rms * norm_gain).astype(jnp.bfloat16)
    logits = jnp.dot(normed, w_router, preferred_element_type=jnp.float32)
    picked = jnp.transpose(routes, (1, 0, 2, 3)).reshape(tok_total, 2)
    onehot = picked[:, :, None] == jnp.arange(EXPERTS, dtype=jnp.int32)[None, None, :]
    chosen = lax.optimization_barrier(jnp.sum(jnp.where(onehot, logits[:, None, :], 0.0), axis=-1))
    combine = jax.nn.sigmoid(chosen)
    cotangent = d_out.reshape(tok_total, D).astype(jnp.float32)
    scaled = (combine[:, :, None] * cotangent[:, None, :]).astype(jnp.bfloat16)
    assign_total = 2 * tok_total
    flag_rows = onehot.reshape(assign_total, EXPERTS).astype(jnp.int32)
    before = jnp.cumsum(flag_rows, axis=0) - flag_rows
    ranking = lax.optimization_barrier(jnp.sum(before * flag_rows, axis=-1)).astype(jnp.int32)
    expert_ids = picked.reshape(-1).astype(jnp.int32)
    bound_rows = DEVICES * CAP
    table = jnp.full((EXPERTS, bound_rows), assign_total, jnp.int32)
    table = table.at[expert_ids, ranking].set(jnp.arange(assign_total, dtype=jnp.int32))
    normed_rows = jnp.concatenate([jnp.repeat(normed, 2, axis=0), jnp.zeros((1, D), jnp.bfloat16)], axis=0)
    scaled_rows = jnp.concatenate([scaled.reshape(assign_total, D), jnp.zeros((1, D), jnp.bfloat16)], axis=0)
    expert_sums, input_sums, gate_grads, up_grads, down_grads = lax.map(expert_pass(normed_rows, scaled_rows), (table, w_gate.reshape(EXPERTS, 2, D, FF // 2), w_up.reshape(EXPERTS, 2, D, FF // 2), w_down.reshape(EXPERTS, 2, FF // 2, D)))
    flat_table = table.reshape(-1)
    expert_outs = jnp.zeros((assign_total + 1, D), jnp.float32).at[flat_table].set(expert_sums.reshape(-1, D))[:assign_total].reshape(tok_total, 2, D)
    d_routed = jnp.zeros((assign_total + 1, D), jnp.float32).at[flat_table].set(input_sums.reshape(-1, D))[:assign_total].reshape(tok_total, 2, D)
    block_sum = hidden_float + lax.optimization_barrier(jnp.sum(combine[:, :, None] * expert_outs, axis=1))
    block_out = block_sum.astype(jnp.bfloat16).reshape(F, P_SIZE, D)
    d_combine = lax.optimization_barrier(jnp.sum(cotangent[:, None, :] * expert_outs, axis=-1))
    d_logit = d_combine * combine * (1.0 - combine)
    router_rows = lax.optimization_barrier(jnp.sum(jnp.where(onehot, d_logit[:, :, None], 0.0), axis=1))
    d_normed = lax.optimization_barrier(jnp.sum(d_routed, axis=1)) + jnp.dot(router_rows, w_router.astype(jnp.float32).T, precision=lax.Precision.HIGHEST)
    gained = d_normed * norm_gain
    d_norm_in = inv_rms * gained - hidden_float * inv_rms ** 3 * lax.optimization_barrier(jnp.mean(gained * hidden_float, axis=-1, keepdims=True))
    d_hidden = (cotangent + d_norm_in).astype(jnp.bfloat16).reshape(F, P_SIZE, D)
    return (block_out, d_hidden, gate_grads.reshape(2 * EXPERTS, D, FF // 2), up_grads.reshape(2 * EXPERTS, D, FF // 2), down_grads.reshape(2 * EXPERTS, FF // 2, D))
```

```python
import functools

import jax
import jax.numpy as jnp
from jax import lax
from jax.experimental import pallas as pl
from jax.experimental.pallas import tpu as pltpu
from jax.sharding import PartitionSpec as P

H = 16
LANES = 128
VM = pltpu.VMEM
BF = jnp.bfloat16
F32 = jnp.float32


def head_windows(width):
    head = width // H
    for h in range(H):
        lo, hi = h * head, (h + 1) * head
        yield lo, hi, lo // LANES * LANES, -(-hi // LANES) * LANES


def attend(q, k, v, out, acc, positions):
    rows, width = q.shape
    scale = (width // H) ** (-0.5)
    at = lax.broadcasted_iota(jnp.int32, (rows, rows), 0) % positions
    other = lax.broadcasted_iota(jnp.int32, (rows, rows), 1) % positions
    same = at == other
    acc[...] = jnp.zeros(acc.shape, F32)
    for lo, hi, w0, w1 in head_windows(width):
        lane = lax.broadcasted_iota(jnp.int32, (rows, w1 - w0), 1) + w0
        mine = (lane >= lo) & (lane < hi)
        zero = jnp.zeros((rows, w1 - w0), BF)
        qh = jnp.where(mine, q[:, w0:w1], zero)
        scores = (
            lax.dot_general(qh, k[:, w0:w1], (((1,), (1,)), ((), ())), preferred_element_type=F32)
            * scale
        )
        scores = jnp.where(same, scores, -1e30)
        weights = jnp.exp(scores - jnp.max(scores, axis=-1, keepdims=True))
        probs = (weights / jnp.sum(weights, axis=-1, keepdims=True)).astype(BF)
        vh = jnp.where(mine, v[:, w0:w1], zero)
        acc[:, w0:w1] += jnp.dot(probs, vh, preferred_element_type=F32)
    out[...] = acc[...].astype(BF)


def attention(q, k, v, positions):
    def body(q_ref, k_ref, v_ref, out_ref, acc):
        attend(q_ref, k_ref, v_ref, out_ref, acc, positions)

    return pl.pallas_call(
        body,
        out_shape=jax.ShapeDtypeStruct(q.shape, BF),
        scratch_shapes=[VM(q.shape, F32)],
    )(q, k, v)


def dot(a, b, ca, cb):
    return lax.dot_general(a, b, (((ca,), (cb,)), ((), ())), preferred_element_type=F32)


def expert_body(x, cot, router, gate, up, down, y, r, d_gate, d_up, d_down):
    xv, cv = x[...], cot[...]
    wr = router[...].astype(F32)
    logit = jnp.sum(xv.astype(F32) * wr, axis=-1, keepdims=True)
    combine = jax.nn.sigmoid(logit)
    cf = cv.astype(F32)
    scaled = (combine * cf).astype(BF)
    pre_gate = dot(xv, gate[...], 1, 0)
    pre_up = dot(xv, up[...], 1, 0)
    sig = jax.nn.sigmoid(pre_gate)
    act = pre_gate * sig
    units = (act * pre_up).astype(BF)
    part = dot(units, down[...], 1, 0).astype(BF).astype(F32)
    y[...] = (combine * part).astype(BF)
    d_units = dot(scaled, down[...], 1, 1)
    dpg = (d_units * pre_up * (sig + act * (1.0 - sig))).astype(BF)
    dpu = (d_units * act).astype(BF)
    d_logit = jnp.sum(cf * part, axis=-1, keepdims=True) * combine * (1.0 - combine)
    d_in = dot(dpg, gate[...], 1, 1) + dot(dpu, up[...], 1, 1)
    r[...] = (d_in + d_logit * wr).astype(BF)
    first = pl.program_id(0) == 0

    @pl.when(first)
    def _():
        d_gate[...] = dot(xv, dpg, 0, 0)
        d_up[...] = dot(xv, dpu, 0, 0)
        d_down[...] = dot(units, scaled, 0, 0)

    @pl.when(jnp.logical_not(first))
    def _():
        d_gate[...] += dot(xv, dpg, 0, 0)
        d_up[...] += dot(xv, dpu, 0, 0)
        d_down[...] += dot(units, scaled, 0, 0)


def expert(x, cot, router, gate, up, down):
    slots, width = x.shape
    hidden = gate.shape[1]
    block = 256 if slots % 256 == 0 else slots
    rows = pl.BlockSpec((block, width), lambda i: (i, 0))

    def whole(shape):
        return pl.BlockSpec(shape, lambda i: (0, 0))

    return pl.pallas_call(
        expert_body,
        grid=(slots // block,),
        in_specs=[rows, rows, whole((1, width)), whole(gate.shape), whole(up.shape), whole(down.shape)],
        out_specs=[rows, rows, whole(gate.shape), whole(up.shape), whole(down.shape)],
        out_shape=[
            jax.ShapeDtypeStruct(x.shape, BF),
            jax.ShapeDtypeStruct(x.shape, BF),
            jax.ShapeDtypeStruct(gate.shape, F32),
            jax.ShapeDtypeStruct(up.shape, F32),
            jax.ShapeDtypeStruct(down.shape, F32),
        ],
        compiler_params=pltpu.CompilerParams(vmem_limit_bytes=60 * 2**20),
    )(x, cot, router, gate, up, down)


def picker(routes_z, expert_count, capacity, frames, depth, z):
    groups, tokens, _ = routes_z.shape
    ids = jnp.arange(expert_count, dtype=jnp.int32)
    onehot = (routes_z[:, :, :, None] == ids).astype(F32).sum(axis=2)
    tri = (jnp.arange(tokens)[:, None] > jnp.arange(tokens)[None, :]).astype(BF)
    before = jnp.einsum("ts,gse->gte", tri, onehot.astype(BF), preferred_element_type=F32)
    mine = frames * depth // 2 // (depth // 2)
    own = (jnp.arange(mine) * (depth // 2)) + z // 2
    hot = jnp.take(onehot, own, axis=2)
    rank = jnp.take(before, own, axis=2)
    place = jnp.where(hot > 0, rank, -1.0).transpose(0, 2, 1)
    slot = jnp.arange(capacity, dtype=F32)
    return (place[:, :, None, :] == slot[None, None, :, None]).astype(BF).reshape(
        groups, mine * capacity, tokens
    )


MESH = pl.DeviceIdType.MESH
ANY = pl.BlockSpec(memory_space=pl.ANY)


def remote(src, dst, send, recv, **to):
    return pltpu.make_async_remote_copy(
        src_ref=src, dst_ref=dst, send_sem=send, recv_sem=recv, device_id=to, device_id_type=MESH
    )


def each_peer(frames, f, fn, first=1, last=None):
    def step(o, carry):
        fn(o, lax.rem(f + o, frames), lax.rem(f + frames - o, frames))
        return carry

    lax.fori_loop(first, last or frames, step, 0)


def greet(frames, depth, f, z):
    barrier = pltpu.get_barrier_semaphore()
    for o in range(1, frames):
        pl.semaphore_signal(
            barrier, inc=1, device_id={"frames": lax.rem(f + o, frames)}, device_id_type=MESH
        )
    for o in range(1, depth):
        pl.semaphore_signal(
            barrier, inc=1, device_id={"expert": lax.rem(z + o, depth)}, device_id_type=MESH
        )
    return lambda: pl.semaphore_wait(barrier, frames + depth - 2)


def turn(k, z):
    if isinstance(k, int):
        return (z, z + 1 - 2 * (z % 2), 2 - z // 2, 3 - 3 * (z // 2))[k]
    near = jnp.where(k == 0, turn(0, z), turn(1, z))
    return jnp.where(k < 2, near, jnp.where(k == 2, turn(2, z), turn(3, z)))


class Relay:
    def __init__(self, depth, z, held, send, recv):
        self.depth, self.z, self.held, self.send, self.recv = depth, z, held, send, recv

    def hop(self, b, up):
        to = jnp.minimum(self.z + 1, self.depth - 1) if up else jnp.maximum(self.z - 1, 0)
        return remote(
            self.held.at[b], self.held.at[b], self.send.at[int(up), b], self.recv.at[b], expert=to
        )

    def pass_on(self, b, fn):
        @pl.when((b <= self.z) & (self.z < self.depth - 1))
        def _():
            fn(self.hop(b, True))

        @pl.when((b >= self.z) & (self.z > 0))
        def _():
            fn(self.hop(b, False))

    def start(self, b):
        self.pass_on(b, lambda c: c.start())

    def arrive(self, b):
        self.hop(b, True).wait_recv()

    def finish(self):
        for b in range(self.depth):
            self.pass_on(b, lambda c: c.wait_send())


def pick_rows(pick, block, frames):
    rows = jnp.dot(pick, block, preferred_element_type=F32).astype(BF)
    return rows.reshape(frames, rows.shape[0] // frames, rows.shape[1])


def tail_body(
    hidden, sums, d_out_in, gain, g0, g1, g2, block_out, d_hidden, o0, o1, o2, d_out, ls, outs,
):
    puts = [
        pltpu.make_async_copy(src, dst, outs.at[i])
        for i, (src, dst) in enumerate(((g0, o0), (g1, o1), (g2, o2)))
    ]
    for c in puts:
        c.start()
    load = pltpu.make_async_copy(d_out_in, d_out, ls)
    load.start()
    hf = hidden[...].astype(F32)
    inv = lax.rsqrt(jnp.mean(hf * hf, axis=-1, keepdims=True) + 1e-06)
    block_out[...] = (hf + sums[0]).astype(BF)
    gained = sums[1] * gain[...].reshape(1, hf.shape[1])
    d_norm_in = inv * gained - hf * (inv * inv * inv) * jnp.mean(gained * hf, axis=-1, keepdims=True)
    load.wait()
    d_hidden[...] = (d_out[...].astype(F32) + d_norm_in).astype(BF)
    for c in puts:
        c.wait()


def tail(hidden, sums, d_out, gain, grads):
    vm = pl.BlockSpec(memory_space=VM)
    dma = pltpu.SemaphoreType.DMA
    kept = [pltpu.with_memory_space_constraint(t, VM) for t in (hidden, sums, *grads)]
    return pl.pallas_call(
        tail_body,
        in_specs=[vm, vm, ANY, vm] + [vm] * 3,
        out_specs=[vm, vm, ANY, ANY, ANY],
        out_shape=[jax.ShapeDtypeStruct(hidden.shape, BF)] * 2
        + [jax.ShapeDtypeStruct(g.shape, F32) for g in grads],
        scratch_shapes=[VM(d_out.shape, d_out.dtype), dma(()), dma((3,))],
        compiler_params=pltpu.CompilerParams(vmem_limit_bytes=32 * 2**20),
    )(kept[0], kept[1], d_out, gain, *kept[2:])


def fused_body(
    frames, depth, q, k, v, d_out_in, routes_in, residual_in, w_out, gain_in, router_in, gate_in, up_in, down_in,
    hidden, sums, d_gate, d_up, d_down,
    routes, residual, gain, router, proj, column, qkv, flat, acc, mix, att, place, pick, d_out, d_across,
    held, cot_slots, out_slots, x, cots,
    gate, up, down, yr, back, part, passed, near, far,
    qs, qr, ats, atr, ps, pr, dsem, zs, zr, cs, cr, es, er, xs, xr, ys, yr_sem, nsem, psem, fsem, ls,
):
    f, z = lax.axis_index("frames"), lax.axis_index("expert")
    _, positions, width = q.shape
    _, _, capacity, _ = x.shape
    tokens = frames * positions
    slots = frames * capacity
    halves = depth // 2
    par = z % 2
    partner = z + 1 - 2 * par
    across = z + halves - 2 * halves * (z // halves)
    met = greet(frames, depth, f, z)
    small = [
        pltpu.make_async_copy(src, dst, ls.at[i])
        for i, (src, dst) in enumerate(
            ((routes_in, routes), (d_out_in, d_out), (router_in, router), (gain_in, gain), (residual_in, residual))
        )
    ]
    own_qkv = [
        pltpu.make_async_copy(t.at[f], qkv.at[i, f], ls.at[5 + i]) for i, t in enumerate((q, k, v))
    ]
    loads = [
        pltpu.make_async_copy(src, dst, ls.at[8 + i])
        for i, (src, dst) in enumerate(((gate_in, gate), (up_in, up), (down_in, down)))
    ]
    project = pltpu.make_async_copy(w_out, proj, ls.at[11])
    for c in small + own_qkv + [project] + loads:
        c.start()
    small[0].wait()
    rows = lax.broadcasted_iota(jnp.int32, (halves * frames, tokens), 0)
    ids = (rows % frames) * halves + rows // frames
    hot = (routes[0:1, :] == ids) | (routes[1:2, :] == ids)
    earlier = lax.broadcasted_iota(jnp.int32, (tokens, tokens), 0)
    later = lax.broadcasted_iota(jnp.int32, (tokens, tokens), 1)
    before = jnp.dot(
        jnp.where(hot, 1.0, 0.0).astype(BF),
        jnp.where(earlier < later, 1.0, 0.0).astype(BF),
        preferred_element_type=F32,
    )
    place[z] = jnp.where(hot, before, -1.0).reshape(halves, frames, tokens)
    slot = lax.broadcasted_iota(jnp.int32, (capacity, tokens), 0).astype(F32)

    def choose(b):
        at = place[b, z // halves]
        for g in range(frames):
            pick[b, g * capacity : (g + 1) * capacity, :] = jnp.where(
                at[g : g + 1, :] == slot, 1.0, 0.0
            ).astype(BF)

    choose(z)
    met()

    def exchange(fn, o, to, source):
        for i, t in enumerate((q, k, v)):
            fn(remote(t.at[to], qkv.at[i, source], qs.at[i, o], qr.at[i, o], frames=to))

    def place_copy(o, source):
        return remote(
            place.at[source], place.at[source], ps.at[o], pr.at[o], expert=lax.rem(z + o, depth)
        )

    def cross_copy():
        return remote(d_out_in, d_across, dsem.at[0], dsem.at[1], expert=across)

    each_peer(frames, f, lambda o, to, fr: exchange(lambda c: c.start(), o, to, f))
    for o in range(1, depth):
        place_copy(o, z).start()
    cross_copy().start()

    def mine(m):
        return across if m else z

    def cot_copy(m, o, to, source):
        return remote(
            cot_slots.at[m, to], cots.at[mine(m), source], cs.at[m, o], cr.at[m, o], frames=to
        )

    def send_cot(m):
        cot_slots[m] = pick_rows(pick[mine(m)], (d_across if m else d_out)[...], frames)
        each_peer(frames, f, lambda o, to, fr: cot_copy(m, o, to, f).start())
        cots[mine(m), f] = cot_slots[m, f]

    def share_copy(m, g):
        piece = cots.at[mine(m), g]
        return remote(piece, piece, es.at[m, g], er.at[m, g], expert=partner)

    def share(m, first, last):
        def step(o, to, fr):
            cot_copy(m, o, to, fr).wait_recv()
            share_copy(m, fr).start()

        each_peer(frames, f, step, first, last)

    def each_frame(fn):
        def step(g, carry):
            fn(g)
            return carry

        lax.fori_loop(0, frames, step, 0)

    small[1].wait()
    send_cot(0)
    small[2].wait()
    expert_ids = lax.broadcasted_iota(jnp.int32, router.shape, 0)
    owned = expert_ids == (f * depth + z) // 2
    column[...] = jnp.sum(jnp.where(owned, router[...].astype(F32), 0.0), axis=0, keepdims=True)
    d_gate[...] = jnp.zeros(d_gate.shape, F32)
    d_up[...] = jnp.zeros(d_up.shape, F32)
    d_down[...] = jnp.zeros(d_down.shape, F32)
    for o in range(1, depth):
        place_copy(o, lax.rem(z + depth - o, depth)).wait_recv()
    for o in range(1, depth):
        choose(lax.rem(z + o, depth))
    for c in own_qkv:
        c.wait()
    each_peer(frames, f, lambda o, to, fr: exchange(lambda c: c.wait_recv(), o, to, fr))
    for i in range(3):
        flat[i] = qkv[i].reshape(tokens, width)
    attend(flat.at[0], flat.at[1], flat.at[2], flat.at[3], acc, positions)
    mix[...] = flat[3].reshape(frames, positions, width)

    def home(o, to, source):
        return remote(mix.at[to], att.at[source], ats.at[o], atr.at[o], frames=to)

    each_peer(frames, f, lambda o, to, fr: home(o, to, f).start())
    att[f] = mix[f]
    cross_copy().wait_recv()
    send_cot(1)
    early = frames // 2
    share_copy(0, f).start()
    share(0, 1, early)
    each_peer(frames, f, lambda o, to, fr: home(o, to, fr).wait_recv())
    for c in [project] + small[3:]:
        c.wait()
    stream = residual[...].astype(F32) + jnp.dot(
        att[...].reshape(tokens, width), proj[...], preferred_element_type=F32
    )
    hid = stream.astype(BF)
    hidden[...] = hid
    hf = hid.astype(F32)
    inv = lax.rsqrt(jnp.mean(hf * hf, axis=-1, keepdims=True) + 1e-06)
    held[z] = (hf * inv * gain[...].reshape(1, width)).astype(BF)

    relay = Relay(depth, z, held, zs, zr)
    relay.start(z)

    def slot_copy(n, o, to, source):
        b = turn(n, z)
        return remote(out_slots.at[b, to], x.at[b, source], xs.at[n, o], xr.at[n, o], frames=to)

    def send_slots(n):
        b = turn(n, z)
        if n:
            relay.arrive(b)
            relay.start(b)
        out_slots[b] = pick_rows(pick[b], held[b], frames)
        each_peer(frames, f, lambda o, to, fr: slot_copy(n, o, to, f).start())
        x[b, f] = out_slots[b, f]

    def result_copy(n, o, to, source):
        b = turn(n, z)
        return remote(yr.at[b, to], back.at[b, source], ys.at[n, o], yr_sem.at[n, o], frames=to)

    def send_results(n):
        b = turn(n, z)
        each_peer(frames, f, lambda o, to, fr: result_copy(n, o, to, f).start())
        back[b, f] = yr[b, f]

    def compute(n):
        b = turn(n, z)
        each_peer(frames, f, lambda o, to, fr: slot_copy(n, o, to, fr).wait_recv())

        @pl.when(n == 1)
        def _():
            each_frame(lambda g: share_copy(0, g).wait_recv())

        @pl.when((n > 1) & (b != across))
        def _():
            each_frame(lambda g: share_copy(1, g).wait_recv())

        xv = x[b].reshape(slots, width)
        cv = cots[b].reshape(slots, width)
        wr = column[...]
        combine = jax.nn.sigmoid(jnp.sum(xv.astype(F32) * wr, axis=-1, keepdims=True))
        cf = cv.astype(F32)
        scaled = (combine * cf).astype(BF)
        pre_gate = dot(xv, gate[...], 1, 0)
        pre_up = dot(xv, up[...], 1, 0)
        sig = jax.nn.sigmoid(pre_gate)
        act = pre_gate * sig
        units = (act * pre_up).astype(BF)
        out = dot(units, down[...], 1, 0).astype(BF).astype(F32)
        yr[b, :, 0] = (combine * out).astype(BF).reshape(frames, capacity, width)
        d_units = dot(scaled, down[...], 1, 1)
        dpg = (d_units * pre_up * (sig + act * (1.0 - sig))).astype(BF)
        dpu = (d_units * act).astype(BF)
        d_logit = jnp.sum(cf * out, axis=-1, keepdims=True) * combine * (1.0 - combine)
        d_in = dot(dpg, gate[...], 1, 1) + dot(dpu, up[...], 1, 1)
        yr[b, :, 1] = (d_in + d_logit * wr).astype(BF).reshape(frames, capacity, width)

        @pl.when(n > 0)
        def _():
            send_results(n)

        d_gate[...] += dot(xv, dpg, 0, 0)
        d_up[...] += dot(xv, dpu, 0, 0)
        d_down[...] += dot(units, scaled, 0, 0)

    def totals(n):
        b = turn(n, z)
        each_peer(frames, f, lambda o, to, fr: result_copy(n, o, to, fr).wait_recv())
        for i in range(2):
            yield dot(pick[b], back[b, :, i].reshape(slots, width), 0, 0)

    outer = (z == 0) | (z == depth - 1)
    opposite = jnp.where(z == halves, halves - 1, halves)

    def inward(n, i):
        return remote(
            part.at[n, i], passed.at[n - 2, i], psem.at[0, n - 2, i], psem.at[1, n - 2, i], expert=partner
        )

    def over(n, i):
        return remote(
            part.at[n, i], far.at[n - 2, i], fsem.at[0, n - 2, i], fsem.at[1, n - 2, i], expert=opposite
        )

    def near_copy(i):
        return remote(part.at[1, i], near.at[i], nsem.at[0, i], nsem.at[1, i], expert=partner)

    def collect(n):
        for i, total in enumerate(totals(n)):
            part[n, i] = total.astype(BF)
            if n > 1:

                @pl.when(outer)
                def _():
                    inward(n, i).start()

    def forward(n):
        @pl.when(jnp.logical_not(outer))
        def _():
            for i in range(2):
                inward(n, i).wait_recv()
                part[n, i] = (part[n, i].astype(F32) + passed[n - 2, i].astype(F32)).astype(BF)
                over(n, i).start()

    def hand_over():
        for i in range(2):

            @pl.when(jnp.logical_not(outer))
            def _():
                over(3, i).wait_recv()
                part[1, i] = (part[1, i].astype(F32) + far[1, i].astype(F32)).astype(BF)

            near_copy(i).start()

    for n in range(depth):
        send_slots(n)
    share_copy(1, f).start()
    share(1, 1, frames)
    share(0, early, frames)
    for c in loads:
        c.wait()

    def step(i, carry):
        compute(jnp.where(i == 0, 0, jnp.where(i == depth - 1, 1, i + 1)))
        return carry

    lax.fori_loop(0, depth, step, 0)
    send_results(0)
    for n in range(2, depth):
        collect(n)
        forward(n)
    collect(1)
    hand_over()
    own = list(totals(0))

    for i in range(2):
        near_copy(i).wait_recv()
        sums[i] = own[i] + near[i].astype(F32)

    @pl.when(jnp.logical_not(outer))
    def _():
        for i in range(2):
            over(2, i).wait_recv()
            sums[i] += far[0, i].astype(F32)

    for i in range(2):
        near_copy(i).wait_send()
        for n in range(2, depth):

            @pl.when(outer)
            def _():
                inward(n, i).wait_send()

            @pl.when(jnp.logical_not(outer))
            def _():
                over(n, i).wait_send()

    for n in range(depth):
        each_peer(frames, f, lambda o, to, fr: slot_copy(n, o, to, f).wait_send())
        each_peer(frames, f, lambda o, to, fr: result_copy(n, o, to, f).wait_send())
    relay.finish()
    cross_copy().wait_send()
    for o in range(1, depth):
        place_copy(o, z).wait_send()
    for m in range(2):
        each_peer(frames, f, lambda o, to, fr: cot_copy(m, o, to, f).wait_send())
        each_frame(lambda g: share_copy(m, g).wait_send())
    each_peer(frames, f, lambda o, to, fr: exchange(lambda c: c.wait_send(), o, to, f))
    each_peer(frames, f, lambda o, to, fr: home(o, to, f).wait_send())


def fused(q, k, v, d_out, routes, residual, w_out, gain, router, gate, up, down, depth, capacity):
    frames, positions, width = q.shape
    tokens = frames * positions
    dma = pltpu.SemaphoreType.DMA
    vm = pl.BlockSpec(memory_space=VM)
    hbm = pl.BlockSpec(memory_space=pltpu.HBM)
    slots = (depth, frames, capacity, width)
    pair = (depth, frames, 2, capacity, width)
    blocks = (depth, tokens, width)
    chunked = (frames, positions, width)
    two = (2, tokens, width)
    return pl.pallas_call(
        functools.partial(fused_body, frames, depth),
        in_specs=[hbm] * 12,
        out_specs=[vm] * 5,
        out_shape=[
            VM((tokens, width), BF),
            VM(two, F32),
            VM(gate.shape, F32),
            VM(up.shape, F32),
            VM(down.shape, F32),
        ],
        scratch_shapes=[
            VM(routes.shape, routes.dtype), VM(residual.shape, BF), VM(gain.shape, F32), VM(router.shape, BF),
            VM(w_out.shape, BF), VM((1, width), F32),
            VM((3,) + chunked, BF), VM((4, tokens, width), BF), VM((tokens, width), F32),
            VM(chunked, BF), VM(chunked, BF),
            VM((depth, depth // 2, frames, tokens), F32),
            VM((depth, frames * capacity, tokens), BF),
            VM((tokens, width), BF), VM((tokens, width), BF), VM(blocks, BF),
            VM((2,) + slots[1:], BF), VM(slots, BF), VM(slots, BF), VM(slots, BF),
            VM(gate.shape, BF), VM(up.shape, BF), VM(down.shape, BF),
            VM(pair, BF), VM(pair, BF),
            VM((depth,) + two, BF), VM((2,) + two, BF), VM(two, BF), VM((2,) + two, BF),
            dma((3, frames)), dma((3, frames)), dma((frames,)), dma((frames,)),
            dma((depth,)), dma((depth,)),
            dma((2,)), dma((2, depth)), dma((depth,)),
            dma((2, frames)), dma((2, frames)), dma((2, frames)), dma((2, frames)),
            dma((depth, frames)), dma((depth, frames)),
            dma((depth, frames)), dma((depth, frames)),
            dma((2, 2)), dma((2, 2, 2)), dma((2, 2, 2)), dma((12,)),
        ],
        compiler_params=pltpu.CompilerParams(
            collective_id=0, has_side_effects=True, vmem_limit_bytes=52 * 2**20
        ),
    )(q, k, v, d_out, routes, residual, w_out, gain, router, gate, up, down)


def on_device(
    residual, queries, keys_in, values, w_out, norm_gain, w_router, routes, w_gate, w_up, w_down, d_out
):
    _, tokens, width = residual.shape
    frames, depth = lax.axis_size("frames"), lax.axis_size("expert")
    f, z = lax.axis_index("frames"), lax.axis_index("expert")
    expert_count = w_router.shape[1]
    capacity = 4 * tokens // expert_count
    positions = tokens // frames

    def across(t):
        return lax.all_to_all(
            t.reshape(frames, -1, width), "frames", split_axis=0, concat_axis=0, tiled=True
        )


    own = (f * depth + z) // 2
    router = lax.dynamic_slice(w_router, (0, own), (width, 1)).reshape(1, width)
    if positions % 16 == 0 and capacity % 16 == 0 and depth == 4:
        rows = d_out.reshape(tokens, width)
        hidden, sums, *grads = fused(
            *(t.reshape(frames, positions, width) for t in (queries, keys_in, values)),
            rows, routes.reshape(tokens, 2).T, residual.reshape(tokens, width), w_out, norm_gain,
            w_router.T, w_gate[0], w_up[0], w_down[0], depth, capacity,
        )
        block_out, d_hidden, *grads = tail(hidden, sums, rows, norm_gain, grads)
        return (
            block_out.reshape(residual.shape), d_hidden.reshape(residual.shape),
            *(g[None] for g in grads),
        )

    routes_z = lax.all_gather(routes.reshape(tokens, 2), "expert", axis=0)
    pick = picker(routes_z, expert_count, capacity, frames, depth, z)
    def dispatch(rows):
        gathered = lax.all_gather(rows, "expert", axis=0)
        picked = jnp.einsum("gst,gtd->gsd", pick, gathered, preferred_element_type=F32).astype(BF)
        picked = picked.reshape(depth, frames, capacity, width).transpose(1, 0, 2, 3)
        return across(picked).reshape(frames * depth * capacity, width)

    q, k, v = (across(t).reshape(tokens, width) for t in (queries, keys_in, values))
    cot = dispatch(d_out.reshape(tokens, width))
    attended = across(attention(q, k, v, positions)).reshape(tokens, width)
    stream = residual.reshape(tokens, width).astype(F32) + jnp.dot(
        attended, w_out, preferred_element_type=F32
    )
    hidden = stream.astype(BF)
    hidden_float = hidden.astype(F32)
    inv_rms = lax.rsqrt(jnp.mean(hidden_float * hidden_float, axis=-1, keepdims=True) + 1e-06)
    normed = (hidden_float * inv_rms * norm_gain).astype(BF)
    x = dispatch(normed)
    y, r, d_gate, d_up, d_down = expert(x, cot, router, w_gate[0], w_up[0], w_down[0])

    def collect(rows):
        back = across(rows).reshape(frames, depth, capacity, width).transpose(1, 0, 2, 3)
        back = back.reshape(depth, frames * capacity, width)
        sums = jnp.einsum("gst,gsd->gtd", pick, back, preferred_element_type=F32).astype(BF)
        return lax.psum_scatter(sums, "expert", scatter_dimension=0, tiled=True)[0].astype(F32)

    expert_sum = collect(y)
    d_normed = collect(r)
    return finish(
        residual, d_out, norm_gain, hidden_float, inv_rms, expert_sum, d_normed, d_gate, d_up, d_down
    )


def finish(
    residual, d_out, norm_gain, hidden_float, inv_rms, expert_sum, d_normed, d_gate, d_up, d_down
):
    cotangent = d_out.reshape(hidden_float.shape).astype(F32)
    block_out = (hidden_float + expert_sum).astype(BF).reshape(residual.shape)
    gained = d_normed * norm_gain
    d_norm_in = inv_rms * gained - hidden_float * inv_rms**3 * jnp.mean(
        gained * hidden_float, axis=-1, keepdims=True
    )
    d_hidden = (cotangent + d_norm_in).astype(BF).reshape(residual.shape)
    return (block_out, d_hidden, d_gate[None], d_up[None], d_down[None])


def solution(mesh):
    tok = P("frames", "expert", None)
    both = P(("frames", "expert"), None, None)
    return jax.shard_map(
        on_device,
        mesh=mesh,
        in_specs=(tok, tok, tok, tok, P(), P(), P(), P("expert", "frames", None, None), both, both, both, tok),
        out_specs=(tok, tok, both, both, both),
        check_vma=False,
    )
```

```python
import functools

import jax
import jax.numpy as jnp
from jax import lax
from jax.experimental import pallas as pl
from jax.experimental.pallas import tpu as pltpu
from jax.sharding import PartitionSpec as P

H = 16
LANES = 128
VM = pltpu.VMEM
BF = jnp.bfloat16
F32 = jnp.float32


def head_windows(width):
    head = width // H
    for h in range(H):
        lo, hi = h * head, (h + 1) * head
        yield lo, hi, lo // LANES * LANES, -(-hi // LANES) * LANES


def attend(q, k, v, out, acc, positions):
    rows, width = q.shape
    scale = (width // H) ** (-0.5)
    at = lax.broadcasted_iota(jnp.int32, (rows, rows), 0) % positions
    other = lax.broadcasted_iota(jnp.int32, (rows, rows), 1) % positions
    same = at == other
    acc[...] = jnp.zeros(acc.shape, F32)
    for lo, hi, w0, w1 in head_windows(width):
        lane = lax.broadcasted_iota(jnp.int32, (rows, w1 - w0), 1) + w0
        mine = (lane >= lo) & (lane < hi)
        zero = jnp.zeros((rows, w1 - w0), BF)
        qh = jnp.where(mine, q[:, w0:w1], zero)
        scores = (
            lax.dot_general(qh, k[:, w0:w1], (((1,), (1,)), ((), ())), preferred_element_type=F32)
            * scale
        )
        scores = jnp.where(same, scores, -1e30)
        weights = jnp.exp(scores - jnp.max(scores, axis=-1, keepdims=True))
        probs = (weights / jnp.sum(weights, axis=-1, keepdims=True)).astype(BF)
        vh = jnp.where(mine, v[:, w0:w1], zero)
        acc[:, w0:w1] += jnp.dot(probs, vh, preferred_element_type=F32)
    out[...] = acc[...].astype(BF)


def attention(q, k, v, positions):
    def body(q_ref, k_ref, v_ref, out_ref, acc):
        attend(q_ref, k_ref, v_ref, out_ref, acc, positions)

    return pl.pallas_call(
        body,
        out_shape=jax.ShapeDtypeStruct(q.shape, BF),
        scratch_shapes=[VM(q.shape, F32)],
    )(q, k, v)


def dot(a, b, ca, cb):
    return lax.dot_general(a, b, (((ca,), (cb,)), ((), ())), preferred_element_type=F32)


def expert_body(x, cot, router, gate, up, down, y, r, d_gate, d_up, d_down):
    xv, cv = x[...], cot[...]
    wr = router[...].astype(F32)
    logit = jnp.sum(xv.astype(F32) * wr, axis=-1, keepdims=True)
    combine = jax.nn.sigmoid(logit)
    cf = cv.astype(F32)
    scaled = (combine * cf).astype(BF)
    pre_gate = dot(xv, gate[...], 1, 0)
    pre_up = dot(xv, up[...], 1, 0)
    sig = jax.nn.sigmoid(pre_gate)
    act = pre_gate * sig
    units = (act * pre_up).astype(BF)
    part = dot(units, down[...], 1, 0).astype(BF).astype(F32)
    y[...] = (combine * part).astype(BF)
    d_units = dot(scaled, down[...], 1, 1)
    dpg = (d_units * pre_up * (sig + act * (1.0 - sig))).astype(BF)
    dpu = (d_units * act).astype(BF)
    d_logit = jnp.sum(cf * part, axis=-1, keepdims=True) * combine * (1.0 - combine)
    d_in = dot(dpg, gate[...], 1, 1) + dot(dpu, up[...], 1, 1)
    r[...] = (d_in + d_logit * wr).astype(BF)
    first = pl.program_id(0) == 0

    @pl.when(first)
    def _():
        d_gate[...] = dot(xv, dpg, 0, 0)
        d_up[...] = dot(xv, dpu, 0, 0)
        d_down[...] = dot(units, scaled, 0, 0)

    @pl.when(jnp.logical_not(first))
    def _():
        d_gate[...] += dot(xv, dpg, 0, 0)
        d_up[...] += dot(xv, dpu, 0, 0)
        d_down[...] += dot(units, scaled, 0, 0)


def expert(x, cot, router, gate, up, down):
    slots, width = x.shape
    hidden = gate.shape[1]
    block = 256 if slots % 256 == 0 else slots
    rows = pl.BlockSpec((block, width), lambda i: (i, 0))

    def whole(shape):
        return pl.BlockSpec(shape, lambda i: (0, 0))

    return pl.pallas_call(
        expert_body,
        grid=(slots // block,),
        in_specs=[rows, rows, whole((1, width)), whole(gate.shape), whole(up.shape), whole(down.shape)],
        out_specs=[rows, rows, whole(gate.shape), whole(up.shape), whole(down.shape)],
        out_shape=[
            jax.ShapeDtypeStruct(x.shape, BF),
            jax.ShapeDtypeStruct(x.shape, BF),
            jax.ShapeDtypeStruct(gate.shape, F32),
            jax.ShapeDtypeStruct(up.shape, F32),
            jax.ShapeDtypeStruct(down.shape, F32),
        ],
        compiler_params=pltpu.CompilerParams(vmem_limit_bytes=60 * 2**20),
    )(x, cot, router, gate, up, down)


def picker(routes_z, expert_count, capacity, frames, depth, z):
    groups, tokens, _ = routes_z.shape
    ids = jnp.arange(expert_count, dtype=jnp.int32)
    onehot = (routes_z[:, :, :, None] == ids).astype(F32).sum(axis=2)
    tri = (jnp.arange(tokens)[:, None] > jnp.arange(tokens)[None, :]).astype(BF)
    before = jnp.einsum("ts,gse->gte", tri, onehot.astype(BF), preferred_element_type=F32)
    mine = frames * depth // 2 // (depth // 2)
    own = (jnp.arange(mine) * (depth // 2)) + z // 2
    hot = jnp.take(onehot, own, axis=2)
    rank = jnp.take(before, own, axis=2)
    place = jnp.where(hot > 0, rank, -1.0).transpose(0, 2, 1)
    slot = jnp.arange(capacity, dtype=F32)
    return (place[:, :, None, :] == slot[None, None, :, None]).astype(BF).reshape(
        groups, mine * capacity, tokens
    )


MESH = pl.DeviceIdType.MESH
ANY = pl.BlockSpec(memory_space=pl.ANY)


def remote(src, dst, send, recv, **to):
    return pltpu.make_async_remote_copy(
        src_ref=src, dst_ref=dst, send_sem=send, recv_sem=recv, device_id=to, device_id_type=MESH
    )


def each_peer(frames, f, fn, first=1, last=None):
    def step(o, carry):
        peer, bit = 0, 1
        while bit < frames:
            low = (f // bit) % 2 + ((frames - o) // bit) % 2
            peer, bit = peer + bit * (low % 2), bit * 2
        fn(o, peer, peer)
        return carry

    lax.fori_loop(first, last or frames, step, 0)


def greet(frames, depth, f, z):
    barrier = pltpu.get_barrier_semaphore()
    for o in range(1, frames):
        pl.semaphore_signal(
            barrier, inc=1, device_id={"frames": lax.rem(f + o, frames)}, device_id_type=MESH
        )
    for o in range(1, depth):
        pl.semaphore_signal(
            barrier, inc=1, device_id={"expert": lax.rem(z + o, depth)}, device_id_type=MESH
        )
    return lambda: pl.semaphore_wait(barrier, frames + depth - 2)


def turn(k, z):
    if isinstance(k, int):
        return (z, z + 1 - 2 * (z % 2), 2 - z // 2, 3 - 3 * (z // 2))[k]
    near = jnp.where(k == 0, turn(0, z), turn(1, z))
    return jnp.where(k < 2, near, jnp.where(k == 2, turn(2, z), turn(3, z)))


class Relay:
    def __init__(self, depth, z, held, send, recv):
        self.depth, self.z, self.held, self.send, self.recv = depth, z, held, send, recv

    def hop(self, b, up):
        to = jnp.minimum(self.z + 1, self.depth - 1) if up else jnp.maximum(self.z - 1, 0)
        return remote(
            self.held.at[b], self.held.at[b], self.send.at[int(up), b], self.recv.at[b], expert=to
        )

    def pass_on(self, b, fn):
        @pl.when((b <= self.z) & (self.z < self.depth - 1))
        def _():
            fn(self.hop(b, True))

        @pl.when((b >= self.z) & (self.z > 0))
        def _():
            fn(self.hop(b, False))

    def start(self, b):
        self.pass_on(b, lambda c: c.start())

    def arrive(self, b):
        self.hop(b, True).wait_recv()

    def finish(self):
        for b in range(self.depth):
            self.pass_on(b, lambda c: c.wait_send())


def pick_rows(pick, block, frames):
    rows = jnp.dot(pick, block, preferred_element_type=F32).astype(BF)
    return rows.reshape(frames, rows.shape[0] // frames, rows.shape[1])


def tail_body(
    hidden, sums, d_out_in, gain, g0, g1, g2, block_out, d_hidden, o0, o1, o2, d_out, ls, outs,
):
    puts = [
        pltpu.make_async_copy(src, dst, outs.at[i])
        for i, (src, dst) in enumerate(((g0, o0), (g1, o1), (g2, o2)))
    ]
    for c in puts:
        c.start()
    load = pltpu.make_async_copy(d_out_in, d_out, ls)
    load.start()
    hf = hidden[...].astype(F32)
    inv = lax.rsqrt(jnp.mean(hf * hf, axis=-1, keepdims=True) + 1e-06)
    block_out[...] = (hf + sums[0]).astype(BF)
    gained = sums[1] * gain[...].reshape(1, hf.shape[1])
    d_norm_in = inv * gained - hf * (inv * inv * inv) * jnp.mean(gained * hf, axis=-1, keepdims=True)
    load.wait()
    d_hidden[...] = (d_out[...].astype(F32) + d_norm_in).astype(BF)
    for c in puts:
        c.wait()


def tail(hidden, sums, d_out, gain, grads):
    vm = pl.BlockSpec(memory_space=VM)
    dma = pltpu.SemaphoreType.DMA
    kept = [pltpu.with_memory_space_constraint(t, VM) for t in (hidden, sums, *grads)]
    return pl.pallas_call(
        tail_body,
        in_specs=[vm, vm, ANY, vm] + [vm] * 3,
        out_specs=[vm, vm, ANY, ANY, ANY],
        out_shape=[jax.ShapeDtypeStruct(hidden.shape, BF)] * 2
        + [jax.ShapeDtypeStruct(g.shape, F32) for g in grads],
        scratch_shapes=[VM(d_out.shape, d_out.dtype), dma(()), dma((3,))],
        compiler_params=pltpu.CompilerParams(vmem_limit_bytes=32 * 2**20),
    )(kept[0], kept[1], d_out, gain, *kept[2:])


def fused_body(
    frames, depth, q, k, v, d_out_in, routes_in, residual_in, w_out, gain_in, router_in, gate_in, up_in, down_in,
    hidden, sums, d_gate, d_up, d_down,
    routes, residual, gain, router, proj, column, qkv, flat, acc, mix, att, place, pick, d_out, d_across,
    held, cot_slots, out_slots, x, cots,
    gate, up, down, yr, back, part, passed, near, far,
    qs, qr, ats, atr, ps, pr, dsem, zs, zr, cs, cr, es, er, xs, xr, ys, yr_sem, nsem, psem, fsem, ls,
):
    f, z = lax.axis_index("frames"), lax.axis_index("expert")
    _, positions, width = q.shape
    _, _, capacity, _ = x.shape
    tokens = frames * positions
    slots = frames * capacity
    halves = depth // 2
    par = z % 2
    partner = z + 1 - 2 * par
    across = z + halves - 2 * halves * (z // halves)
    met = greet(frames, depth, f, z)
    small = [
        pltpu.make_async_copy(src, dst, ls.at[i])
        for i, (src, dst) in enumerate(
            ((routes_in, routes), (d_out_in, d_out), (router_in, router), (gain_in, gain), (residual_in, residual))
        )
    ]
    own_qkv = [
        pltpu.make_async_copy(t.at[f], qkv.at[i, f], ls.at[5 + i]) for i, t in enumerate((q, k, v))
    ]
    loads = [
        pltpu.make_async_copy(src, dst, ls.at[8 + i])
        for i, (src, dst) in enumerate(((gate_in, gate), (up_in, up), (down_in, down)))
    ]
    project = pltpu.make_async_copy(w_out, proj, ls.at[11])
    for c in small + own_qkv + [project] + loads:
        c.start()
    small[0].wait()
    rows = lax.broadcasted_iota(jnp.int32, (halves * frames, tokens), 0)
    ids = (rows % frames) * halves + rows // frames
    hot = (routes[0:1, :] == ids) | (routes[1:2, :] == ids)
    earlier = lax.broadcasted_iota(jnp.int32, (tokens, tokens), 0)
    later = lax.broadcasted_iota(jnp.int32, (tokens, tokens), 1)
    before = jnp.dot(
        jnp.where(hot, 1.0, 0.0).astype(BF),
        jnp.where(earlier < later, 1.0, 0.0).astype(BF),
        preferred_element_type=F32,
    )
    place[z] = jnp.where(hot, before, -1.0).reshape(halves, frames, tokens)
    slot = lax.broadcasted_iota(jnp.int32, (capacity, tokens), 0).astype(F32)

    def choose(b):
        at = place[b, z // halves]
        for g in range(frames):
            pick[b, g * capacity : (g + 1) * capacity, :] = jnp.where(
                at[g : g + 1, :] == slot, 1.0, 0.0
            ).astype(BF)

    choose(z)
    met()

    def exchange(fn, o, to, source):
        for i, t in enumerate((q, k, v)):
            fn(remote(t.at[to], qkv.at[i, source], qs.at[i, o], qr.at[i, o], frames=to))

    def place_copy(o, source):
        return remote(
            place.at[source], place.at[source], ps.at[o], pr.at[o], expert=lax.rem(z + o, depth)
        )

    def cross_copy():
        return remote(d_out_in, d_across, dsem.at[0], dsem.at[1], expert=across)

    each_peer(frames, f, lambda o, to, fr: exchange(lambda c: c.start(), o, to, f))
    for o in range(1, depth):
        place_copy(o, z).start()
    cross_copy().start()

    def mine(m):
        return across if m else z

    def cot_copy(m, o, to, source):
        return remote(
            cot_slots.at[m, to], cots.at[mine(m), source], cs.at[m, o], cr.at[m, o], frames=to
        )

    def send_cot(m):
        cot_slots[m] = pick_rows(pick[mine(m)], (d_across if m else d_out)[...], frames)
        each_peer(frames, f, lambda o, to, fr: cot_copy(m, o, to, f).start())
        cots[mine(m), f] = cot_slots[m, f]

    def share_copy(m, g):
        piece = cots.at[mine(m), g]
        return remote(piece, piece, es.at[m, g], er.at[m, g], expert=partner)

    def share(m, first, last):
        def step(o, to, fr):
            cot_copy(m, o, to, fr).wait_recv()
            share_copy(m, fr).start()

        each_peer(frames, f, step, first, last)

    def each_frame(fn):
        def step(g, carry):
            fn(g)
            return carry

        lax.fori_loop(0, frames, step, 0)

    small[1].wait()
    send_cot(0)
    small[2].wait()
    expert_ids = lax.broadcasted_iota(jnp.int32, router.shape, 0)
    owned = expert_ids == (f * depth + z) // 2
    column[...] = jnp.sum(jnp.where(owned, router[...].astype(F32), 0.0), axis=0, keepdims=True)
    d_gate[...] = jnp.zeros(d_gate.shape, F32)
    d_up[...] = jnp.zeros(d_up.shape, F32)
    d_down[...] = jnp.zeros(d_down.shape, F32)
    for o in range(1, depth):
        place_copy(o, lax.rem(z + depth - o, depth)).wait_recv()
    for o in range(1, depth):
        choose(lax.rem(z + o, depth))
    for c in own_qkv:
        c.wait()
    each_peer(frames, f, lambda o, to, fr: exchange(lambda c: c.wait_recv(), o, to, fr))
    for i in range(3):
        flat[i] = qkv[i].reshape(tokens, width)
    attend(flat.at[0], flat.at[1], flat.at[2], flat.at[3], acc, positions)
    mix[...] = flat[3].reshape(frames, positions, width)

    def home(o, to, source):
        return remote(mix.at[to], att.at[source], ats.at[o], atr.at[o], frames=to)

    each_peer(frames, f, lambda o, to, fr: home(o, to, f).start())
    att[f] = mix[f]
    cross_copy().wait_recv()
    send_cot(1)
    early = frames // 2
    share_copy(0, f).start()
    share(0, 1, early)
    each_peer(frames, f, lambda o, to, fr: home(o, to, fr).wait_recv())
    for c in [project] + small[3:]:
        c.wait()
    stream = residual[...].astype(F32) + jnp.dot(
        att[...].reshape(tokens, width), proj[...], preferred_element_type=F32
    )
    hid = stream.astype(BF)
    hidden[...] = hid
    hf = hid.astype(F32)
    inv = lax.rsqrt(jnp.mean(hf * hf, axis=-1, keepdims=True) + 1e-06)
    held[z] = (hf * inv * gain[...].reshape(1, width)).astype(BF)

    relay = Relay(depth, z, held, zs, zr)
    relay.start(z)

    def slot_copy(n, o, to, source):
        b = turn(n, z)
        return remote(out_slots.at[b, to], x.at[b, source], xs.at[n, o], xr.at[n, o], frames=to)

    def send_slots(n):
        b = turn(n, z)
        if n:
            relay.arrive(b)
            relay.start(b)
        out_slots[b] = pick_rows(pick[b], held[b], frames)
        each_peer(frames, f, lambda o, to, fr: slot_copy(n, o, to, f).start())
        x[b, f] = out_slots[b, f]

    def result_copy(n, i, o, to, source):
        b = turn(n, z)
        return remote(
            yr.at[b, i, to], back.at[b, i, source], ys.at[n, i, o], yr_sem.at[n, i, o], frames=to
        )

    def send_results(n, i):
        b = turn(n, z)
        each_peer(frames, f, lambda o, to, fr: result_copy(n, i, o, to, f).start())
        back[b, i, f] = yr[b, i, f]

    def compute(n):
        b = turn(n, z)
        each_peer(frames, f, lambda o, to, fr: slot_copy(n, o, to, fr).wait_recv())

        @pl.when(n == 1)
        def _():
            each_frame(lambda g: share_copy(0, g).wait_recv())

        @pl.when((n > 1) & (b != across))
        def _():
            each_frame(lambda g: share_copy(1, g).wait_recv())

        xv = x[b].reshape(slots, width)
        cv = cots[b].reshape(slots, width)
        wr = column[...]
        combine = jax.nn.sigmoid(jnp.sum(xv.astype(F32) * wr, axis=-1, keepdims=True))
        cf = cv.astype(F32)
        scaled = (combine * cf).astype(BF)
        pre_gate = dot(xv, gate[...], 1, 0)
        pre_up = dot(xv, up[...], 1, 0)
        sig = jax.nn.sigmoid(pre_gate)
        act = pre_gate * sig
        units = (act * pre_up).astype(BF)
        out = dot(units, down[...], 1, 0).astype(BF).astype(F32)
        yr[b, 0] = (combine * out).astype(BF).reshape(frames, capacity, width)

        @pl.when(n > 0)
        def _():
            send_results(n, 0)

        d_units = dot(scaled, down[...], 1, 1)
        dpg = (d_units * pre_up * (sig + act * (1.0 - sig))).astype(BF)
        dpu = (d_units * act).astype(BF)
        d_logit = jnp.sum(cf * out, axis=-1, keepdims=True) * combine * (1.0 - combine)
        d_in = dot(dpg, gate[...], 1, 1) + dot(dpu, up[...], 1, 1)
        yr[b, 1] = (d_in + d_logit * wr).astype(BF).reshape(frames, capacity, width)

        @pl.when(n > 0)
        def _():
            send_results(n, 1)

        d_gate[...] += dot(xv, dpg, 0, 0)
        d_up[...] += dot(xv, dpu, 0, 0)
        d_down[...] += dot(units, scaled, 0, 0)

    def totals(n):
        b = turn(n, z)
        for i in range(2):
            each_peer(frames, f, lambda o, to, fr: result_copy(n, i, o, to, fr).wait_recv())
            yield dot(pick[b], back[b, i].reshape(slots, width), 0, 0)

    outer = (z == 0) | (z == depth - 1)
    opposite = jnp.where(z == halves, halves - 1, halves)

    def inward(n, i):
        return remote(
            part.at[n, i], passed.at[n - 2, i], psem.at[0, n - 2, i], psem.at[1, n - 2, i], expert=partner
        )

    def over(n, i):
        return remote(
            part.at[n, i], far.at[n - 2, i], fsem.at[0, n - 2, i], fsem.at[1, n - 2, i], expert=opposite
        )

    def near_copy(i):
        return remote(part.at[1, i], near.at[i], nsem.at[0, i], nsem.at[1, i], expert=partner)

    def collect(n):
        for i, total in enumerate(totals(n)):
            part[n, i] = total.astype(BF)

            @pl.when(outer)
            def _():
                inward(n, i).start()

    def forward(n):
        @pl.when(jnp.logical_not(outer))
        def _():
            for i in range(2):
                inward(n, i).wait_recv()
                part[n, i] = (part[n, i].astype(F32) + passed[n - 2, i].astype(F32)).astype(BF)
                over(n, i).start()

    def hand_over():
        for i, total in enumerate(totals(1)):

            @pl.when(outer)
            def _():
                part[1, i] = total.astype(BF)

            @pl.when(jnp.logical_not(outer))
            def _():
                over(3, i).wait_recv()
                part[1, i] = (total + far[1, i].astype(F32)).astype(BF)

            near_copy(i).start()

    def share_rest():
        share_copy(1, f).start()
        share(1, 1, frames)
        share(0, early, frames)

    send_slots(0)

    @pl.when(outer)
    def _():
        share_rest()

    for n in range(1, depth):
        send_slots(n)

    @pl.when(jnp.logical_not(outer))
    def _():
        share_rest()

    for c in loads:
        c.wait()

    def step(i, carry):
        compute(jnp.where(i == 0, 0, jnp.where(i == depth - 1, 1, i + 1)))
        return carry

    lax.fori_loop(0, depth, step, 0)
    for i in range(2):
        send_results(0, i)
    for n in range(depth):
        each_peer(frames, f, lambda o, to, fr: slot_copy(n, o, to, f).wait_send())
    relay.finish()
    cross_copy().wait_send()
    for o in range(1, depth):
        place_copy(o, z).wait_send()
    for m in range(2):
        each_peer(frames, f, lambda o, to, fr: cot_copy(m, o, to, f).wait_send())
        each_frame(lambda g: share_copy(m, g).wait_send())
    each_peer(frames, f, lambda o, to, fr: exchange(lambda c: c.wait_send(), o, to, f))
    each_peer(frames, f, lambda o, to, fr: home(o, to, f).wait_send())
    for n in range(2, depth):
        collect(n)
        forward(n)
    hand_over()
    own = list(totals(0))

    for i in range(2):
        near_copy(i).wait_recv()
        sums[i] = own[i] + near[i].astype(F32)

    @pl.when(jnp.logical_not(outer))
    def _():
        for i in range(2):
            over(2, i).wait_recv()
            sums[i] += far[0, i].astype(F32)

    for i in range(2):
        near_copy(i).wait_send()
        for n in range(2, depth):

            @pl.when(outer)
            def _():
                inward(n, i).wait_send()

            @pl.when(jnp.logical_not(outer))
            def _():
                over(n, i).wait_send()

    for n in range(depth):
        for i in range(2):
            each_peer(frames, f, lambda o, to, fr: result_copy(n, i, o, to, f).wait_send())


def fused(q, k, v, d_out, routes, residual, w_out, gain, router, gate, up, down, depth, capacity):
    frames, positions, width = q.shape
    tokens = frames * positions
    dma = pltpu.SemaphoreType.DMA
    vm = pl.BlockSpec(memory_space=VM)
    hbm = pl.BlockSpec(memory_space=pltpu.HBM)
    slots = (depth, frames, capacity, width)
    pair = (depth, 2, frames, capacity, width)
    blocks = (depth, tokens, width)
    chunked = (frames, positions, width)
    two = (2, tokens, width)
    return pl.pallas_call(
        functools.partial(fused_body, frames, depth),
        in_specs=[hbm] * 12,
        out_specs=[vm] * 5,
        out_shape=[
            VM((tokens, width), BF),
            VM(two, F32),
            VM(gate.shape, F32),
            VM(up.shape, F32),
            VM(down.shape, F32),
        ],
        scratch_shapes=[
            VM(routes.shape, routes.dtype), VM(residual.shape, BF), VM(gain.shape, F32), VM(router.shape, BF),
            VM(w_out.shape, BF), VM((1, width), F32),
            VM((3,) + chunked, BF), VM((4, tokens, width), BF), VM((tokens, width), F32),
            VM(chunked, BF), VM(chunked, BF),
            VM((depth, depth // 2, frames, tokens), F32),
            VM((depth, frames * capacity, tokens), BF),
            VM((tokens, width), BF), VM((tokens, width), BF), VM(blocks, BF),
            VM((2,) + slots[1:], BF), VM(slots, BF), VM(slots, BF), VM(slots, BF),
            VM(gate.shape, BF), VM(up.shape, BF), VM(down.shape, BF),
            VM(pair, BF), VM(pair, BF),
            VM((depth,) + two, BF), VM((2,) + two, BF), VM(two, BF), VM((2,) + two, BF),
            dma((3, frames)), dma((3, frames)), dma((frames,)), dma((frames,)),
            dma((depth,)), dma((depth,)),
            dma((2,)), dma((2, depth)), dma((depth,)),
            dma((2, frames)), dma((2, frames)), dma((2, frames)), dma((2, frames)),
            dma((depth, frames)), dma((depth, frames)),
            dma((depth, 2, frames)), dma((depth, 2, frames)),
            dma((2, 2)), dma((2, 2, 2)), dma((2, 2, 2)), dma((12,)),
        ],
        compiler_params=pltpu.CompilerParams(
            collective_id=0, has_side_effects=True, vmem_limit_bytes=52 * 2**20
        ),
    )(q, k, v, d_out, routes, residual, w_out, gain, router, gate, up, down)


def on_device(
    residual, queries, keys_in, values, w_out, norm_gain, w_router, routes, w_gate, w_up, w_down, d_out
):
    _, tokens, width = residual.shape
    frames, depth = lax.axis_size("frames"), lax.axis_size("expert")
    f, z = lax.axis_index("frames"), lax.axis_index("expert")
    expert_count = w_router.shape[1]
    capacity = 4 * tokens // expert_count
    positions = tokens // frames

    def across(t):
        return lax.all_to_all(
            t.reshape(frames, -1, width), "frames", split_axis=0, concat_axis=0, tiled=True
        )


    own = (f * depth + z) // 2
    router = lax.dynamic_slice(w_router, (0, own), (width, 1)).reshape(1, width)
    if positions % 16 == 0 and capacity % 16 == 0 and depth == 4 and frames & (frames - 1) == 0:
        rows = d_out.reshape(tokens, width)
        hidden, sums, *grads = fused(
            *(t.reshape(frames, positions, width) for t in (queries, keys_in, values)),
            rows, routes.reshape(tokens, 2).T, residual.reshape(tokens, width), w_out, norm_gain,
            w_router.T, w_gate[0], w_up[0], w_down[0], depth, capacity,
        )
        block_out, d_hidden, *grads = tail(hidden, sums, rows, norm_gain, grads)
        return (
            block_out.reshape(residual.shape), d_hidden.reshape(residual.shape),
            *(g[None] for g in grads),
        )

    routes_z = lax.all_gather(routes.reshape(tokens, 2), "expert", axis=0)
    pick = picker(routes_z, expert_count, capacity, frames, depth, z)
    def dispatch(rows):
        gathered = lax.all_gather(rows, "expert", axis=0)
        picked = jnp.einsum("gst,gtd->gsd", pick, gathered, preferred_element_type=F32).astype(BF)
        picked = picked.reshape(depth, frames, capacity, width).transpose(1, 0, 2, 3)
        return across(picked).reshape(frames * depth * capacity, width)

    q, k, v = (across(t).reshape(tokens, width) for t in (queries, keys_in, values))
    cot = dispatch(d_out.reshape(tokens, width))
    attended = across(attention(q, k, v, positions)).reshape(tokens, width)
    stream = residual.reshape(tokens, width).astype(F32) + jnp.dot(
        attended, w_out, preferred_element_type=F32
    )
    hidden = stream.astype(BF)
    hidden_float = hidden.astype(F32)
    inv_rms = lax.rsqrt(jnp.mean(hidden_float * hidden_float, axis=-1, keepdims=True) + 1e-06)
    normed = (hidden_float * inv_rms * norm_gain).astype(BF)
    x = dispatch(normed)
    y, r, d_gate, d_up, d_down = expert(x, cot, router, w_gate[0], w_up[0], w_down[0])

    def collect(rows):
        back = across(rows).reshape(frames, depth, capacity, width).transpose(1, 0, 2, 3)
        back = back.reshape(depth, frames * capacity, width)
        sums = jnp.einsum("gst,gsd->gtd", pick, back, preferred_element_type=F32).astype(BF)
        return lax.psum_scatter(sums, "expert", scatter_dimension=0, tiled=True)[0].astype(F32)

    expert_sum = collect(y)
    d_normed = collect(r)
    return finish(
        residual, d_out, norm_gain, hidden_float, inv_rms, expert_sum, d_normed, d_gate, d_up, d_down
    )


def finish(
    residual, d_out, norm_gain, hidden_float, inv_rms, expert_sum, d_normed, d_gate, d_up, d_down
):
    cotangent = d_out.reshape(hidden_float.shape).astype(F32)
    block_out = (hidden_float + expert_sum).astype(BF).reshape(residual.shape)
    gained = d_normed * norm_gain
    d_norm_in = inv_rms * gained - hidden_float * inv_rms**3 * jnp.mean(
        gained * hidden_float, axis=-1, keepdims=True
    )
    d_hidden = (cotangent + d_norm_in).astype(BF).reshape(residual.shape)
    return (block_out, d_hidden, d_gate[None], d_up[None], d_down[None])


def solution(mesh):
    tok = P("frames", "expert", None)
    both = P(("frames", "expert"), None, None)
    return jax.shard_map(
        on_device,
        mesh=mesh,
        in_specs=(tok, tok, tok, tok, P(), P(), P(), P("expert", "frames", None, None), both, both, both, tok),
        out_specs=(tok, tok, both, both, both),
        check_vma=False,
    )
```

```python
import functools

import jax
import jax.numpy as jnp
from jax import lax
from jax.experimental import pallas as pl
from jax.experimental.pallas import tpu as pltpu
from jax.sharding import PartitionSpec as P

H = 16
LANES = 128
VM = pltpu.VMEM
BF = jnp.bfloat16
F32 = jnp.float32


def head_windows(width):
    head = width // H
    for h in range(H):
        lo, hi = h * head, (h + 1) * head
        yield lo, hi, lo // LANES * LANES, -(-hi // LANES) * LANES


def attend(q, k, v, out, acc, positions):
    rows, width = q.shape
    scale = (width // H) ** (-0.5)
    at = lax.broadcasted_iota(jnp.int32, (rows, rows), 0) % positions
    other = lax.broadcasted_iota(jnp.int32, (rows, rows), 1) % positions
    same = at == other
    acc[...] = jnp.zeros(acc.shape, F32)
    for lo, hi, w0, w1 in head_windows(width):
        lane = lax.broadcasted_iota(jnp.int32, (rows, w1 - w0), 1) + w0
        mine = (lane >= lo) & (lane < hi)
        zero = jnp.zeros((rows, w1 - w0), BF)
        qh = jnp.where(mine, q[:, w0:w1], zero)
        scores = (
            lax.dot_general(qh, k[:, w0:w1], (((1,), (1,)), ((), ())), preferred_element_type=F32)
            * scale
        )
        scores = jnp.where(same, scores, -1e30)
        weights = jnp.exp(scores - jnp.max(scores, axis=-1, keepdims=True))
        probs = (weights / jnp.sum(weights, axis=-1, keepdims=True)).astype(BF)
        vh = jnp.where(mine, v[:, w0:w1], zero)
        acc[:, w0:w1] += jnp.dot(probs, vh, preferred_element_type=F32)
    out[...] = acc[...].astype(BF)


def attention(q, k, v, positions):
    def body(q_ref, k_ref, v_ref, out_ref, acc):
        attend(q_ref, k_ref, v_ref, out_ref, acc, positions)

    return pl.pallas_call(
        body,
        out_shape=jax.ShapeDtypeStruct(q.shape, BF),
        scratch_shapes=[VM(q.shape, F32)],
    )(q, k, v)


def dot(a, b, ca, cb):
    return lax.dot_general(a, b, (((ca,), (cb,)), ((), ())), preferred_element_type=F32)


def expert_body(x, cot, router, gate, up, down, y, r, d_gate, d_up, d_down):
    xv, cv = x[...], cot[...]
    wr = router[...].astype(F32)
    logit = jnp.sum(xv.astype(F32) * wr, axis=-1, keepdims=True)
    combine = jax.nn.sigmoid(logit)
    cf = cv.astype(F32)
    scaled = (combine * cf).astype(BF)
    pre_gate = dot(xv, gate[...], 1, 0)
    pre_up = dot(xv, up[...], 1, 0)
    sig = jax.nn.sigmoid(pre_gate)
    act = pre_gate * sig
    units = (act * pre_up).astype(BF)
    part = dot(units, down[...], 1, 0).astype(BF).astype(F32)
    y[...] = (combine * part).astype(BF)
    d_units = dot(scaled, down[...], 1, 1)
    dpg = (d_units * pre_up * (sig + act * (1.0 - sig))).astype(BF)
    dpu = (d_units * act).astype(BF)
    d_logit = jnp.sum(cf * part, axis=-1, keepdims=True) * combine * (1.0 - combine)
    d_in = dot(dpg, gate[...], 1, 1) + dot(dpu, up[...], 1, 1)
    r[...] = (d_in + d_logit * wr).astype(BF)
    first = pl.program_id(0) == 0

    @pl.when(first)
    def _():
        d_gate[...] = dot(xv, dpg, 0, 0)
        d_up[...] = dot(xv, dpu, 0, 0)
        d_down[...] = dot(units, scaled, 0, 0)

    @pl.when(jnp.logical_not(first))
    def _():
        d_gate[...] += dot(xv, dpg, 0, 0)
        d_up[...] += dot(xv, dpu, 0, 0)
        d_down[...] += dot(units, scaled, 0, 0)


def expert(x, cot, router, gate, up, down):
    slots, width = x.shape
    hidden = gate.shape[1]
    block = 256 if slots % 256 == 0 else slots
    rows = pl.BlockSpec((block, width), lambda i: (i, 0))

    def whole(shape):
        return pl.BlockSpec(shape, lambda i: (0, 0))

    return pl.pallas_call(
        expert_body,
        grid=(slots // block,),
        in_specs=[rows, rows, whole((1, width)), whole(gate.shape), whole(up.shape), whole(down.shape)],
        out_specs=[rows, rows, whole(gate.shape), whole(up.shape), whole(down.shape)],
        out_shape=[
            jax.ShapeDtypeStruct(x.shape, BF),
            jax.ShapeDtypeStruct(x.shape, BF),
            jax.ShapeDtypeStruct(gate.shape, F32),
            jax.ShapeDtypeStruct(up.shape, F32),
            jax.ShapeDtypeStruct(down.shape, F32),
        ],
        compiler_params=pltpu.CompilerParams(vmem_limit_bytes=60 * 2**20),
    )(x, cot, router, gate, up, down)


def picker(routes_z, expert_count, capacity, frames, depth, z):
    groups, tokens, _ = routes_z.shape
    ids = jnp.arange(expert_count, dtype=jnp.int32)
    onehot = (routes_z[:, :, :, None] == ids).astype(F32).sum(axis=2)
    tri = (jnp.arange(tokens)[:, None] > jnp.arange(tokens)[None, :]).astype(BF)
    before = jnp.einsum("ts,gse->gte", tri, onehot.astype(BF), preferred_element_type=F32)
    mine = frames * depth // 2 // (depth // 2)
    own = (jnp.arange(mine) * (depth // 2)) + z // 2
    hot = jnp.take(onehot, own, axis=2)
    rank = jnp.take(before, own, axis=2)
    place = jnp.where(hot > 0, rank, -1.0).transpose(0, 2, 1)
    slot = jnp.arange(capacity, dtype=F32)
    return (place[:, :, None, :] == slot[None, None, :, None]).astype(BF).reshape(
        groups, mine * capacity, tokens
    )


MESH = pl.DeviceIdType.MESH
ANY = pl.BlockSpec(memory_space=pl.ANY)


def remote(src, dst, send, recv, **to):
    return pltpu.make_async_remote_copy(
        src_ref=src, dst_ref=dst, send_sem=send, recv_sem=recv, device_id=to, device_id_type=MESH
    )


def each_peer(frames, f, fn, first=1, last=None):
    def step(o, carry):
        peer, bit = 0, 1
        while bit < frames:
            low = (f // bit) % 2 + ((frames - o) // bit) % 2
            peer, bit = peer + bit * (low % 2), bit * 2
        fn(o, peer, peer)
        return carry

    lax.fori_loop(first, last or frames, step, 0)


def greet(frames, depth, f, z):
    barrier = pltpu.get_barrier_semaphore()
    for o in range(1, frames):
        pl.semaphore_signal(
            barrier, inc=1, device_id={"frames": lax.rem(f + o, frames)}, device_id_type=MESH
        )
    for o in range(1, depth):
        pl.semaphore_signal(
            barrier, inc=1, device_id={"expert": lax.rem(z + o, depth)}, device_id_type=MESH
        )
    return lambda: pl.semaphore_wait(barrier, frames + depth - 2)


def turn(k, z):
    if isinstance(k, int):
        return (z, z + 1 - 2 * (z % 2), 2 - z // 2, 3 - 3 * (z // 2))[k]
    near = jnp.where(k == 0, turn(0, z), turn(1, z))
    return jnp.where(k < 2, near, jnp.where(k == 2, turn(2, z), turn(3, z)))


class Relay:
    def __init__(self, depth, z, held, send, recv):
        self.depth, self.z, self.held, self.send, self.recv = depth, z, held, send, recv

    def hop(self, b, up):
        to = jnp.minimum(self.z + 1, self.depth - 1) if up else jnp.maximum(self.z - 1, 0)
        return remote(
            self.held.at[b], self.held.at[b], self.send.at[int(up), b], self.recv.at[b], expert=to
        )

    def pass_on(self, b, fn):
        @pl.when((b <= self.z) & (self.z < self.depth - 1))
        def _():
            fn(self.hop(b, True))

        @pl.when((b >= self.z) & (self.z > 0))
        def _():
            fn(self.hop(b, False))

    def start(self, b):
        self.pass_on(b, lambda c: c.start())

    def arrive(self, b):
        self.hop(b, True).wait_recv()

    def finish(self):
        for b in range(self.depth):
            self.pass_on(b, lambda c: c.wait_send())


def pick_rows(pick, block, frames):
    rows = jnp.dot(pick, block, preferred_element_type=F32).astype(BF)
    return rows.reshape(frames, rows.shape[0] // frames, rows.shape[1])


def tail_body(
    hidden, sums, d_out_in, gain, g0, g1, g2, block_out, d_hidden, o0, o1, o2, d_out, first, second, ls, outs,
):
    puts = [
        pltpu.make_async_copy(src, dst, outs.at[i])
        for i, (src, dst) in enumerate(
            ((g0, o0), (g1, o1), (g2, o2), (first, block_out), (second, d_hidden))
        )
    ]
    for c in puts[:3]:
        c.start()
    load = pltpu.make_async_copy(d_out_in, d_out, ls)
    load.start()
    hf = hidden[...].astype(F32)
    inv = lax.rsqrt(jnp.mean(hf * hf, axis=-1, keepdims=True) + 1e-06)
    first[...] = (hf + sums[0]).astype(BF)
    puts[3].start()
    gained = sums[1] * gain[...].reshape(1, hf.shape[1])
    d_norm_in = inv * gained - hf * (inv * inv * inv) * jnp.mean(gained * hf, axis=-1, keepdims=True)
    load.wait()
    second[...] = (d_out[...].astype(F32) + d_norm_in).astype(BF)
    puts[4].start()
    for c in puts:
        c.wait()


def tail(hidden, sums, d_out, gain, grads):
    vm = pl.BlockSpec(memory_space=VM)
    dma = pltpu.SemaphoreType.DMA
    kept = [pltpu.with_memory_space_constraint(t, VM) for t in (hidden, sums, *grads)]
    return pl.pallas_call(
        tail_body,
        in_specs=[vm, vm, ANY, vm] + [vm] * 3,
        out_specs=[ANY] * 5,
        out_shape=[jax.ShapeDtypeStruct(hidden.shape, BF)] * 2
        + [jax.ShapeDtypeStruct(g.shape, F32) for g in grads],
        scratch_shapes=[VM(d_out.shape, BF)] * 3 + [dma(()), dma((5,))],
        compiler_params=pltpu.CompilerParams(vmem_limit_bytes=32 * 2**20),
    )(kept[0], kept[1], d_out, gain, *kept[2:])


def fused_body(
    frames, depth, q, k, v, d_out_in, routes_in, residual_in, w_out, gain_in, router_in, gate_in, up_in, down_in,
    hidden, sums, d_gate, d_up, d_down,
    routes, residual, gain, router, proj, column, qkv, flat, acc, mix, att, place, pick, d_out, d_across,
    held, cot_slots, out_slots, x, cots,
    gate, up, down, yr, back, part, passed, near, far,
    qs, qr, ats, atr, ps, pr, dsem, zs, zr, cs, cr, es, er, xs, xr, ys, yr_sem, nsem, psem, fsem, ls,
):
    f, z = lax.axis_index("frames"), lax.axis_index("expert")
    _, positions, width = q.shape
    _, _, capacity, _ = x.shape
    tokens = frames * positions
    slots = frames * capacity
    halves = depth // 2
    par = z % 2
    partner = z + 1 - 2 * par
    across = z + halves - 2 * halves * (z // halves)
    met = greet(frames, depth, f, z)
    small = [
        pltpu.make_async_copy(src, dst, ls.at[i])
        for i, (src, dst) in enumerate(
            ((routes_in, routes), (d_out_in, d_out), (router_in, router), (gain_in, gain), (residual_in, residual))
        )
    ]
    own_qkv = [
        pltpu.make_async_copy(t.at[f], qkv.at[i, f], ls.at[5 + i]) for i, t in enumerate((q, k, v))
    ]
    loads = [
        pltpu.make_async_copy(src, dst, ls.at[8 + i])
        for i, (src, dst) in enumerate(((gate_in, gate), (up_in, up), (down_in, down)))
    ]
    project = pltpu.make_async_copy(w_out, proj, ls.at[11])
    for c in small + own_qkv + [project] + loads:
        c.start()
    small[0].wait()
    rows = lax.broadcasted_iota(jnp.int32, (halves * frames, tokens), 0)
    ids = (rows % frames) * halves + rows // frames
    hot = (routes[0:1, :] == ids) | (routes[1:2, :] == ids)
    earlier = lax.broadcasted_iota(jnp.int32, (tokens, tokens), 0)
    later = lax.broadcasted_iota(jnp.int32, (tokens, tokens), 1)
    before = jnp.dot(
        jnp.where(hot, 1.0, 0.0).astype(BF),
        jnp.where(earlier < later, 1.0, 0.0).astype(BF),
        preferred_element_type=F32,
    )
    place[z] = jnp.where(hot, before, -1.0).reshape(halves, frames, tokens)
    slot = lax.broadcasted_iota(jnp.int32, (capacity, tokens), 0).astype(F32)

    def choose(b):
        at = place[b, z // halves]
        for g in range(frames):
            pick[b, g * capacity : (g + 1) * capacity, :] = jnp.where(
                at[g : g + 1, :] == slot, 1.0, 0.0
            ).astype(BF)

    choose(z)
    met()

    def exchange(fn, o, to, source):
        for i, t in enumerate((q, k, v)):
            fn(remote(t.at[to], qkv.at[i, source], qs.at[i, o], qr.at[i, o], frames=to))

    def place_copy(o, source):
        return remote(
            place.at[source], place.at[source], ps.at[o], pr.at[o], expert=lax.rem(z + o, depth)
        )

    def cross_copy():
        return remote(d_out_in, d_across, dsem.at[0], dsem.at[1], expert=across)

    each_peer(frames, f, lambda o, to, fr: exchange(lambda c: c.start(), o, to, f))
    for o in range(1, depth):
        place_copy(o, z).start()
    cross_copy().start()

    def mine(m):
        return across if m else z

    def cot_copy(m, o, to, source):
        return remote(
            cot_slots.at[m, to], cots.at[mine(m), source], cs.at[m, o], cr.at[m, o], frames=to
        )

    def send_cot(m):
        cot_slots[m] = pick_rows(pick[mine(m)], (d_across if m else d_out)[...], frames)
        each_peer(frames, f, lambda o, to, fr: cot_copy(m, o, to, f).start())
        cots[mine(m), f] = cot_slots[m, f]

    def share_copy(m, g):
        piece = cots.at[mine(m), g]
        return remote(piece, piece, es.at[m, g], er.at[m, g], expert=partner)

    def share(m, first, last):
        def step(o, to, fr):
            cot_copy(m, o, to, fr).wait_recv()
            share_copy(m, fr).start()

        each_peer(frames, f, step, first, last)

    def each_frame(fn):
        def step(g, carry):
            fn(g)
            return carry

        lax.fori_loop(0, frames, step, 0)

    small[1].wait()
    send_cot(0)
    small[2].wait()
    expert_ids = lax.broadcasted_iota(jnp.int32, router.shape, 0)
    owned = expert_ids == (f * depth + z) // 2
    column[...] = jnp.sum(jnp.where(owned, router[...].astype(F32), 0.0), axis=0, keepdims=True)
    d_gate[...] = jnp.zeros(d_gate.shape, F32)
    d_up[...] = jnp.zeros(d_up.shape, F32)
    d_down[...] = jnp.zeros(d_down.shape, F32)
    for o in range(1, depth):
        place_copy(o, lax.rem(z + depth - o, depth)).wait_recv()
    for o in range(1, depth):
        choose(lax.rem(z + o, depth))
    for c in own_qkv:
        c.wait()
    each_peer(frames, f, lambda o, to, fr: exchange(lambda c: c.wait_recv(), o, to, fr))
    for i in range(3):
        flat[i] = qkv[i].reshape(tokens, width)
    attend(flat.at[0], flat.at[1], flat.at[2], flat.at[3], acc, positions)
    mix[...] = flat[3].reshape(frames, positions, width)

    def home(o, to, source):
        return remote(mix.at[to], att.at[source], ats.at[o], atr.at[o], frames=to)

    each_peer(frames, f, lambda o, to, fr: home(o, to, f).start())
    att[f] = mix[f]
    cross_copy().wait_recv()
    send_cot(1)
    early = frames // 2
    share_copy(0, f).start()
    share(0, 1, early)
    each_peer(frames, f, lambda o, to, fr: home(o, to, fr).wait_recv())
    for c in [project] + small[3:]:
        c.wait()
    stream = residual[...].astype(F32) + jnp.dot(
        att[...].reshape(tokens, width), proj[...], preferred_element_type=F32
    )
    hid = stream.astype(BF)
    hidden[...] = hid
    hf = hid.astype(F32)
    inv = lax.rsqrt(jnp.mean(hf * hf, axis=-1, keepdims=True) + 1e-06)
    held[z] = (hf * inv * gain[...].reshape(1, width)).astype(BF)

    relay = Relay(depth, z, held, zs, zr)
    relay.start(z)

    def slot_copy(n, o, to, source):
        b = turn(n, z)
        return remote(out_slots.at[b, to], x.at[b, source], xs.at[n, o], xr.at[n, o], frames=to)

    def send_slots(n):
        b = turn(n, z)
        if n:
            relay.arrive(b)
            relay.start(b)
        out_slots[b] = pick_rows(pick[b], held[b], frames)
        each_peer(frames, f, lambda o, to, fr: slot_copy(n, o, to, f).start())
        x[b, f] = out_slots[b, f]

    def result_copy(n, i, o, to, source):
        b = turn(n, z)
        return remote(
            yr.at[b, i, to], back.at[b, i, source], ys.at[n, i, o], yr_sem.at[n, i, o], frames=to
        )

    def send_results(n, i):
        b = turn(n, z)
        each_peer(frames, f, lambda o, to, fr: result_copy(n, i, o, to, f).start())
        back[b, i, f] = yr[b, i, f]

    def compute(n):
        b = turn(n, z)
        each_peer(frames, f, lambda o, to, fr: slot_copy(n, o, to, fr).wait_recv())

        @pl.when(n == 1)
        def _():
            each_frame(lambda g: share_copy(0, g).wait_recv())

        @pl.when((n > 1) & (b != across))
        def _():
            each_frame(lambda g: share_copy(1, g).wait_recv())

        xv = x[b].reshape(slots, width)
        cv = cots[b].reshape(slots, width)
        wr = column[...]
        combine = jax.nn.sigmoid(jnp.sum(xv.astype(F32) * wr, axis=-1, keepdims=True))
        cf = cv.astype(F32)
        scaled = (combine * cf).astype(BF)
        pre_gate = dot(xv, gate[...], 1, 0)
        pre_up = dot(xv, up[...], 1, 0)
        sig = jax.nn.sigmoid(pre_gate)
        act = pre_gate * sig
        units = (act * pre_up).astype(BF)
        out = dot(units, down[...], 1, 0).astype(BF).astype(F32)
        yr[b, 0] = (combine * out).astype(BF).reshape(frames, capacity, width)

        @pl.when(n > 0)
        def _():
            send_results(n, 0)

        d_units = dot(scaled, down[...], 1, 1)
        dpg = (d_units * pre_up * (sig + act * (1.0 - sig))).astype(BF)
        dpu = (d_units * act).astype(BF)
        d_logit = jnp.sum(cf * out, axis=-1, keepdims=True) * combine * (1.0 - combine)
        d_in = dot(dpg, gate[...], 1, 1) + dot(dpu, up[...], 1, 1)
        yr[b, 1] = (d_in + d_logit * wr).astype(BF).reshape(frames, capacity, width)

        @pl.when(n > 0)
        def _():
            send_results(n, 1)

        d_gate[...] += dot(xv, dpg, 0, 0)
        d_up[...] += dot(xv, dpu, 0, 0)
        d_down[...] += dot(units, scaled, 0, 0)

    def totals(n):
        b = turn(n, z)
        for i in range(2):
            each_peer(frames, f, lambda o, to, fr: result_copy(n, i, o, to, fr).wait_recv())
            yield dot(pick[b], back[b, i].reshape(slots, width), 0, 0)

    outer = (z == 0) | (z == depth - 1)
    opposite = jnp.where(z == halves, halves - 1, halves)

    def inward(n, i):
        return remote(
            part.at[n, i], passed.at[n - 2, i], psem.at[0, n - 2, i], psem.at[1, n - 2, i], expert=partner
        )

    def over(n, i):
        return remote(
            part.at[n, i], far.at[n - 2, i], fsem.at[0, n - 2, i], fsem.at[1, n - 2, i], expert=opposite
        )

    def near_copy(i):
        return remote(part.at[1, i], near.at[i], nsem.at[0, i], nsem.at[1, i], expert=partner)

    def collect(n):
        for i, total in enumerate(totals(n)):
            part[n, i] = total.astype(BF)

            @pl.when(outer)
            def _():
                inward(n, i).start()

    def forward(n):
        @pl.when(jnp.logical_not(outer))
        def _():
            for i in range(2):
                inward(n, i).wait_recv()
                part[n, i] = (part[n, i].astype(F32) + passed[n - 2, i].astype(F32)).astype(BF)
                over(n, i).start()

    def hand_over():
        for i, total in enumerate(totals(1)):

            @pl.when(outer)
            def _():
                part[1, i] = total.astype(BF)

            @pl.when(jnp.logical_not(outer))
            def _():
                over(3, i).wait_recv()
                part[1, i] = (total + far[1, i].astype(F32)).astype(BF)

            near_copy(i).start()

    def share_rest():
        share_copy(1, f).start()
        share(1, 1, frames)
        share(0, early, frames)

    send_slots(0)

    @pl.when(outer)
    def _():
        share_rest()

    for n in range(1, depth):
        send_slots(n)

    @pl.when(jnp.logical_not(outer))
    def _():
        share_rest()

    for c in loads:
        c.wait()

    def step(i, carry):
        @pl.when(i == depth - 1)
        def _():
            collect(2)

        compute(jnp.where(i == 0, 0, jnp.where(i == depth - 1, 1, i + 1)))
        return carry

    lax.fori_loop(0, depth, step, 0)
    for i in range(2):
        send_results(0, i)
    for n in range(depth):
        each_peer(frames, f, lambda o, to, fr: slot_copy(n, o, to, f).wait_send())
    relay.finish()
    cross_copy().wait_send()
    for o in range(1, depth):
        place_copy(o, z).wait_send()
    for m in range(2):
        each_peer(frames, f, lambda o, to, fr: cot_copy(m, o, to, f).wait_send())
        each_frame(lambda g: share_copy(m, g).wait_send())
    each_peer(frames, f, lambda o, to, fr: exchange(lambda c: c.wait_send(), o, to, f))
    each_peer(frames, f, lambda o, to, fr: home(o, to, f).wait_send())
    forward(2)
    collect(3)
    forward(3)
    hand_over()
    own = list(totals(0))

    for i in range(2):
        near_copy(i).wait_recv()
        sums[i] = own[i] + near[i].astype(F32)

    @pl.when(jnp.logical_not(outer))
    def _():
        for i in range(2):
            over(2, i).wait_recv()
            sums[i] += far[0, i].astype(F32)

    for i in range(2):
        near_copy(i).wait_send()
        for n in range(2, depth):

            @pl.when(outer)
            def _():
                inward(n, i).wait_send()

            @pl.when(jnp.logical_not(outer))
            def _():
                over(n, i).wait_send()

    for n in range(depth):
        for i in range(2):
            each_peer(frames, f, lambda o, to, fr: result_copy(n, i, o, to, f).wait_send())


def fused(q, k, v, d_out, routes, residual, w_out, gain, router, gate, up, down, depth, capacity):
    frames, positions, width = q.shape
    tokens = frames * positions
    dma = pltpu.SemaphoreType.DMA
    vm = pl.BlockSpec(memory_space=VM)
    hbm = pl.BlockSpec(memory_space=pltpu.HBM)
    slots = (depth, frames, capacity, width)
    pair = (depth, 2, frames, capacity, width)
    blocks = (depth, tokens, width)
    chunked = (frames, positions, width)
    two = (2, tokens, width)
    return pl.pallas_call(
        functools.partial(fused_body, frames, depth),
        in_specs=[hbm] * 12,
        out_specs=[vm] * 5,
        out_shape=[
            VM((tokens, width), BF),
            VM(two, F32),
            VM(gate.shape, F32),
            VM(up.shape, F32),
            VM(down.shape, F32),
        ],
        scratch_shapes=[
            VM(routes.shape, routes.dtype), VM(residual.shape, BF), VM(gain.shape, F32), VM(router.shape, BF),
            VM(w_out.shape, BF), VM((1, width), F32),
            VM((3,) + chunked, BF), VM((4, tokens, width), BF), VM((tokens, width), F32),
            VM(chunked, BF), VM(chunked, BF),
            VM((depth, depth // 2, frames, tokens), F32),
            VM((depth, frames * capacity, tokens), BF),
            VM((tokens, width), BF), VM((tokens, width), BF), VM(blocks, BF),
            VM((2,) + slots[1:], BF), VM(slots, BF), VM(slots, BF), VM(slots, BF),
            VM(gate.shape, BF), VM(up.shape, BF), VM(down.shape, BF),
            VM(pair, BF), VM(pair, BF),
            VM((depth,) + two, BF), VM((2,) + two, BF), VM(two, BF), VM((2,) + two, BF),
            dma((3, frames)), dma((3, frames)), dma((frames,)), dma((frames,)),
            dma((depth,)), dma((depth,)),
            dma((2,)), dma((2, depth)), dma((depth,)),
            dma((2, frames)), dma((2, frames)), dma((2, frames)), dma((2, frames)),
            dma((depth, frames)), dma((depth, frames)),
            dma((depth, 2, frames)), dma((depth, 2, frames)),
            dma((2, 2)), dma((2, 2, 2)), dma((2, 2, 2)), dma((12,)),
        ],
        compiler_params=pltpu.CompilerParams(
            collective_id=0, has_side_effects=True, vmem_limit_bytes=52 * 2**20
        ),
    )(q, k, v, d_out, routes, residual, w_out, gain, router, gate, up, down)


def on_device(
    residual, queries, keys_in, values, w_out, norm_gain, w_router, routes, w_gate, w_up, w_down, d_out
):
    _, tokens, width = residual.shape
    frames, depth = lax.axis_size("frames"), lax.axis_size("expert")
    f, z = lax.axis_index("frames"), lax.axis_index("expert")
    expert_count = w_router.shape[1]
    capacity = 4 * tokens // expert_count
    positions = tokens // frames

    def across(t):
        return lax.all_to_all(
            t.reshape(frames, -1, width), "frames", split_axis=0, concat_axis=0, tiled=True
        )


    own = (f * depth + z) // 2
    router = lax.dynamic_slice(w_router, (0, own), (width, 1)).reshape(1, width)
    if positions % 16 == 0 and capacity % 16 == 0 and depth == 4 and frames & (frames - 1) == 0:
        rows = d_out.reshape(tokens, width)
        hidden, sums, *grads = fused(
            *(t.reshape(frames, positions, width) for t in (queries, keys_in, values)),
            rows, routes.reshape(tokens, 2).T, residual.reshape(tokens, width), w_out, norm_gain,
            w_router.T, w_gate[0], w_up[0], w_down[0], depth, capacity,
        )
        block_out, d_hidden, *grads = tail(hidden, sums, rows, norm_gain, grads)
        return (
            block_out.reshape(residual.shape), d_hidden.reshape(residual.shape),
            *(g[None] for g in grads),
        )

    routes_z = lax.all_gather(routes.reshape(tokens, 2), "expert", axis=0)
    pick = picker(routes_z, expert_count, capacity, frames, depth, z)
    def dispatch(rows):
        gathered = lax.all_gather(rows, "expert", axis=0)
        picked = jnp.einsum("gst,gtd->gsd", pick, gathered, preferred_element_type=F32).astype(BF)
        picked = picked.reshape(depth, frames, capacity, width).transpose(1, 0, 2, 3)
        return across(picked).reshape(frames * depth * capacity, width)

    q, k, v = (across(t).reshape(tokens, width) for t in (queries, keys_in, values))
    cot = dispatch(d_out.reshape(tokens, width))
    attended = across(attention(q, k, v, positions)).reshape(tokens, width)
    stream = residual.reshape(tokens, width).astype(F32) + jnp.dot(
        attended, w_out, preferred_element_type=F32
    )
    hidden = stream.astype(BF)
    hidden_float = hidden.astype(F32)
    inv_rms = lax.rsqrt(jnp.mean(hidden_float * hidden_float, axis=-1, keepdims=True) + 1e-06)
    normed = (hidden_float * inv_rms * norm_gain).astype(BF)
    x = dispatch(normed)
    y, r, d_gate, d_up, d_down = expert(x, cot, router, w_gate[0], w_up[0], w_down[0])

    def collect(rows):
        back = across(rows).reshape(frames, depth, capacity, width).transpose(1, 0, 2, 3)
        back = back.reshape(depth, frames * capacity, width)
        sums = jnp.einsum("gst,gsd->gtd", pick, back, preferred_element_type=F32).astype(BF)
        return lax.psum_scatter(sums, "expert", scatter_dimension=0, tiled=True)[0].astype(F32)

    expert_sum = collect(y)
    d_normed = collect(r)
    return finish(
        residual, d_out, norm_gain, hidden_float, inv_rms, expert_sum, d_normed, d_gate, d_up, d_down
    )


def finish(
    residual, d_out, norm_gain, hidden_float, inv_rms, expert_sum, d_normed, d_gate, d_up, d_down
):
    cotangent = d_out.reshape(hidden_float.shape).astype(F32)
    block_out = (hidden_float + expert_sum).astype(BF).reshape(residual.shape)
    gained = d_normed * norm_gain
    d_norm_in = inv_rms * gained - hidden_float * inv_rms**3 * jnp.mean(
        gained * hidden_float, axis=-1, keepdims=True
    )
    d_hidden = (cotangent + d_norm_in).astype(BF).reshape(residual.shape)
    return (block_out, d_hidden, d_gate[None], d_up[None], d_down[None])


def solution(mesh):
    tok = P("frames", "expert", None)
    both = P(("frames", "expert"), None, None)
    return jax.shard_map(
        on_device,
        mesh=mesh,
        in_specs=(tok, tok, tok, tok, P(), P(), P(), P("expert", "frames", None, None), both, both, both, tok),
        out_specs=(tok, tok, both, both, both),
        check_vma=False,
    )
```

```python
import functools

import jax
import jax.numpy as jnp
from jax import lax
from jax.experimental import pallas as pl
from jax.experimental.pallas import tpu as pltpu
from jax.sharding import PartitionSpec as P

H = 16
LANES = 128
VM = pltpu.VMEM
BF = jnp.bfloat16
F32 = jnp.float32


def head_windows(width):
    head = width // H
    for h in range(H):
        lo, hi = h * head, (h + 1) * head
        yield lo, hi, lo // LANES * LANES, -(-hi // LANES) * LANES


def attend(q, k, v, out, acc, positions):
    rows, width = q.shape
    scale = (width // H) ** (-0.5)
    at = lax.broadcasted_iota(jnp.int32, (rows, rows), 0) % positions
    other = lax.broadcasted_iota(jnp.int32, (rows, rows), 1) % positions
    same = at == other
    acc[...] = jnp.zeros(acc.shape, F32)
    for lo, hi, w0, w1 in head_windows(width):
        lane = lax.broadcasted_iota(jnp.int32, (rows, w1 - w0), 1) + w0
        mine = (lane >= lo) & (lane < hi)
        zero = jnp.zeros((rows, w1 - w0), BF)
        qh = jnp.where(mine, q[:, w0:w1], zero)
        scores = (
            lax.dot_general(qh, k[:, w0:w1], (((1,), (1,)), ((), ())), preferred_element_type=F32)
            * scale
        )
        scores = jnp.where(same, scores, -1e30)
        weights = jnp.exp(scores - jnp.max(scores, axis=-1, keepdims=True))
        probs = (weights / jnp.sum(weights, axis=-1, keepdims=True)).astype(BF)
        vh = jnp.where(mine, v[:, w0:w1], zero)
        acc[:, w0:w1] += jnp.dot(probs, vh, preferred_element_type=F32)
    out[...] = acc[...].astype(BF)


def attention(q, k, v, positions):
    def body(q_ref, k_ref, v_ref, out_ref, acc):
        attend(q_ref, k_ref, v_ref, out_ref, acc, positions)

    return pl.pallas_call(
        body,
        out_shape=jax.ShapeDtypeStruct(q.shape, BF),
        scratch_shapes=[VM(q.shape, F32)],
    )(q, k, v)


def dot(a, b, ca, cb):
    return lax.dot_general(a, b, (((ca,), (cb,)), ((), ())), preferred_element_type=F32)


def expert_body(x, cot, router, gate, up, down, y, r, d_gate, d_up, d_down):
    xv, cv = x[...], cot[...]
    wr = router[...].astype(F32)
    logit = jnp.sum(xv.astype(F32) * wr, axis=-1, keepdims=True)
    combine = jax.nn.sigmoid(logit)
    cf = cv.astype(F32)
    scaled = (combine * cf).astype(BF)
    pre_gate = dot(xv, gate[...], 1, 0)
    pre_up = dot(xv, up[...], 1, 0)
    sig = jax.nn.sigmoid(pre_gate)
    act = pre_gate * sig
    units = (act * pre_up).astype(BF)
    part = dot(units, down[...], 1, 0).astype(BF).astype(F32)
    y[...] = (combine * part).astype(BF)
    d_units = dot(scaled, down[...], 1, 1)
    dpg = (d_units * pre_up * (sig + act * (1.0 - sig))).astype(BF)
    dpu = (d_units * act).astype(BF)
    d_logit = jnp.sum(cf * part, axis=-1, keepdims=True) * combine * (1.0 - combine)
    d_in = dot(dpg, gate[...], 1, 1) + dot(dpu, up[...], 1, 1)
    r[...] = (d_in + d_logit * wr).astype(BF)
    first = pl.program_id(0) == 0

    @pl.when(first)
    def _():
        d_gate[...] = dot(xv, dpg, 0, 0)
        d_up[...] = dot(xv, dpu, 0, 0)
        d_down[...] = dot(units, scaled, 0, 0)

    @pl.when(jnp.logical_not(first))
    def _():
        d_gate[...] += dot(xv, dpg, 0, 0)
        d_up[...] += dot(xv, dpu, 0, 0)
        d_down[...] += dot(units, scaled, 0, 0)


def expert(x, cot, router, gate, up, down):
    slots, width = x.shape
    hidden = gate.shape[1]
    block = 256 if slots % 256 == 0 else slots
    rows = pl.BlockSpec((block, width), lambda i: (i, 0))

    def whole(shape):
        return pl.BlockSpec(shape, lambda i: (0, 0))

    return pl.pallas_call(
        expert_body,
        grid=(slots // block,),
        in_specs=[rows, rows, whole((1, width)), whole(gate.shape), whole(up.shape), whole(down.shape)],
        out_specs=[rows, rows, whole(gate.shape), whole(up.shape), whole(down.shape)],
        out_shape=[
            jax.ShapeDtypeStruct(x.shape, BF),
            jax.ShapeDtypeStruct(x.shape, BF),
            jax.ShapeDtypeStruct(gate.shape, F32),
            jax.ShapeDtypeStruct(up.shape, F32),
            jax.ShapeDtypeStruct(down.shape, F32),
        ],
        compiler_params=pltpu.CompilerParams(vmem_limit_bytes=60 * 2**20),
    )(x, cot, router, gate, up, down)


def picker(routes_z, expert_count, capacity, frames, depth, z):
    groups, tokens, _ = routes_z.shape
    ids = jnp.arange(expert_count, dtype=jnp.int32)
    onehot = (routes_z[:, :, :, None] == ids).astype(F32).sum(axis=2)
    tri = (jnp.arange(tokens)[:, None] > jnp.arange(tokens)[None, :]).astype(BF)
    before = jnp.einsum("ts,gse->gte", tri, onehot.astype(BF), preferred_element_type=F32)
    mine = frames * depth // 2 // (depth // 2)
    own = (jnp.arange(mine) * (depth // 2)) + z // 2
    hot = jnp.take(onehot, own, axis=2)
    rank = jnp.take(before, own, axis=2)
    place = jnp.where(hot > 0, rank, -1.0).transpose(0, 2, 1)
    slot = jnp.arange(capacity, dtype=F32)
    return (place[:, :, None, :] == slot[None, None, :, None]).astype(BF).reshape(
        groups, mine * capacity, tokens
    )


MESH = pl.DeviceIdType.MESH
ANY = pl.BlockSpec(memory_space=pl.ANY)


def remote(src, dst, send, recv, **to):
    return pltpu.make_async_remote_copy(
        src_ref=src, dst_ref=dst, send_sem=send, recv_sem=recv, device_id=to, device_id_type=MESH
    )


def each_peer(frames, f, fn, first=1, last=None):
    def step(o, carry):
        peer, bit = 0, 1
        while bit < frames:
            low = (f // bit) % 2 + ((frames - o) // bit) % 2
            peer, bit = peer + bit * (low % 2), bit * 2
        fn(o, peer, peer)
        return carry

    lax.fori_loop(first, last or frames, step, 0)


def greet(frames, depth, f, z):
    barrier = pltpu.get_barrier_semaphore()
    for o in range(1, frames):
        pl.semaphore_signal(
            barrier, inc=1, device_id={"frames": lax.rem(f + o, frames)}, device_id_type=MESH
        )
    for o in range(1, depth):
        pl.semaphore_signal(
            barrier, inc=1, device_id={"expert": lax.rem(z + o, depth)}, device_id_type=MESH
        )
    return lambda: pl.semaphore_wait(barrier, frames + depth - 2)


def turn(k, z):
    if isinstance(k, int):
        return (z, z + 1 - 2 * (z % 2), 2 - z // 2, 3 - 3 * (z // 2))[k]
    near = jnp.where(k == 0, turn(0, z), turn(1, z))
    return jnp.where(k < 2, near, jnp.where(k == 2, turn(2, z), turn(3, z)))


class Relay:
    def __init__(self, depth, z, held, send, recv):
        self.depth, self.z, self.held, self.send, self.recv = depth, z, held, send, recv

    def hop(self, b, up):
        to = jnp.minimum(self.z + 1, self.depth - 1) if up else jnp.maximum(self.z - 1, 0)
        return remote(
            self.held.at[b], self.held.at[b], self.send.at[int(up), b], self.recv.at[b], expert=to
        )

    def pass_on(self, b, fn):
        @pl.when((b <= self.z) & (self.z < self.depth - 1))
        def _():
            fn(self.hop(b, True))

        @pl.when((b >= self.z) & (self.z > 0))
        def _():
            fn(self.hop(b, False))

    def start(self, b):
        self.pass_on(b, lambda c: c.start())

    def arrive(self, b):
        self.hop(b, True).wait_recv()

    def finish(self):
        for b in range(self.depth):
            self.pass_on(b, lambda c: c.wait_send())


def pick_rows(pick, block, frames):
    rows = jnp.dot(pick, block, preferred_element_type=F32).astype(BF)
    return rows.reshape(frames, rows.shape[0] // frames, rows.shape[1])


def tail_body(
    hidden, sums, d_out_in, gain, g0, g1, g2, block_out, d_hidden, o0, o1, o2, d_out, first, second, ls, outs,
):
    puts = [
        pltpu.make_async_copy(src, dst, outs.at[i])
        for i, (src, dst) in enumerate(
            ((g0, o0), (g1, o1), (g2, o2), (first, block_out), (second, d_hidden))
        )
    ]
    for c in puts[:3]:
        c.start()
    load = pltpu.make_async_copy(d_out_in, d_out, ls)
    load.start()
    hf = hidden[...].astype(F32)
    inv = lax.rsqrt(jnp.mean(hf * hf, axis=-1, keepdims=True) + 1e-06)
    first[...] = (hf + sums[0]).astype(BF)
    puts[3].start()
    gained = sums[1] * gain[...].reshape(1, hf.shape[1])
    d_norm_in = inv * gained - hf * (inv * inv * inv) * jnp.mean(gained * hf, axis=-1, keepdims=True)
    load.wait()
    second[...] = (d_out[...].astype(F32) + d_norm_in).astype(BF)
    puts[4].start()
    for c in puts:
        c.wait()


def tail(hidden, sums, d_out, gain, grads):
    vm = pl.BlockSpec(memory_space=VM)
    dma = pltpu.SemaphoreType.DMA
    kept = [pltpu.with_memory_space_constraint(t, VM) for t in (hidden, sums, *grads)]
    return pl.pallas_call(
        tail_body,
        in_specs=[vm, vm, ANY, vm] + [vm] * 3,
        out_specs=[ANY] * 5,
        out_shape=[jax.ShapeDtypeStruct(hidden.shape, BF)] * 2
        + [jax.ShapeDtypeStruct(g.shape, F32) for g in grads],
        scratch_shapes=[VM(d_out.shape, BF)] * 3 + [dma(()), dma((5,))],
        compiler_params=pltpu.CompilerParams(vmem_limit_bytes=32 * 2**20),
    )(kept[0], kept[1], d_out, gain, *kept[2:])


def fused_body(
    frames, depth, q, k, v, d_out_in, routes_in, residual_in, w_out, gain_in, router_in, gate_in, up_in, down_in,
    hidden, sums, d_gate, d_up, d_down,
    routes, residual, gain, router, proj, column, qkv, flat, acc, mix, att, place, pick, d_out, d_across,
    held, cot_slots, out_slots, x, cots,
    gate, up, down, yr, back, part, passed, near, far,
    qs, qr, ats, atr, ps, pr, dsem, zs, zr, cs, cr, es, er, hs, hr, xs, xr, ys, yr_sem, nsem, psem, fsem, ls,
):
    f, z = lax.axis_index("frames"), lax.axis_index("expert")
    _, positions, width = q.shape
    _, _, capacity, _ = x.shape
    tokens = frames * positions
    slots = frames * capacity
    halves = depth // 2
    par = z % 2
    partner = z + 1 - 2 * par
    across = z + halves - 2 * halves * (z // halves)
    cut = frames // 4 + 1
    met = greet(frames, depth, f, z)
    small = [
        pltpu.make_async_copy(src, dst, ls.at[i])
        for i, (src, dst) in enumerate(
            ((routes_in, routes), (d_out_in, d_out), (router_in, router), (gain_in, gain), (residual_in, residual))
        )
    ]
    own_qkv = [
        pltpu.make_async_copy(t.at[f], qkv.at[i, f], ls.at[5 + i]) for i, t in enumerate((q, k, v))
    ]
    loads = [
        pltpu.make_async_copy(src, dst, ls.at[8 + i])
        for i, (src, dst) in enumerate(((gate_in, gate), (up_in, up), (down_in, down)))
    ]
    project = pltpu.make_async_copy(w_out, proj, ls.at[11])
    for c in small + own_qkv + [project] + loads:
        c.start()
    small[0].wait()
    rows = lax.broadcasted_iota(jnp.int32, (halves * frames, tokens), 0)
    ids = (rows % frames) * halves + rows // frames
    hot = (routes[0:1, :] == ids) | (routes[1:2, :] == ids)
    earlier = lax.broadcasted_iota(jnp.int32, (tokens, tokens), 0)
    later = lax.broadcasted_iota(jnp.int32, (tokens, tokens), 1)
    before = jnp.dot(
        jnp.where(hot, 1.0, 0.0).astype(BF),
        jnp.where(earlier < later, 1.0, 0.0).astype(BF),
        preferred_element_type=F32,
    )
    place[z] = jnp.where(hot, before, -1.0).reshape(halves, frames, tokens)
    slot = lax.broadcasted_iota(jnp.int32, (capacity, tokens), 0).astype(F32)

    def choose(b):
        at = place[b, z // halves]
        for g in range(frames):
            pick[b, g * capacity : (g + 1) * capacity, :] = jnp.where(
                at[g : g + 1, :] == slot, 1.0, 0.0
            ).astype(BF)

    choose(z)
    met()

    def exchange(fn, o, to, source):
        for i, t in enumerate((q, k, v)):
            fn(remote(t.at[to], qkv.at[i, source], qs.at[i, o], qr.at[i, o], frames=to))

    def place_copy(o, source):
        return remote(
            place.at[source], place.at[source], ps.at[o], pr.at[o], expert=lax.rem(z + o, depth)
        )

    def cross_copy():
        return remote(d_out_in, d_across, dsem.at[0], dsem.at[1], expert=across)

    each_peer(frames, f, lambda o, to, fr: exchange(lambda c: c.start(), o, to, f))
    for o in range(1, depth):
        place_copy(o, z).start()
    cross_copy().start()

    def mine(m):
        return across if m else z

    def cot_copy(m, o, to, source):
        return remote(
            cot_slots.at[m, to], cots.at[mine(m), source], cs.at[m, o], cr.at[m, o], frames=to
        )

    def send_cot(m):
        cot_slots[m] = pick_rows(pick[mine(m)], (d_across if m else d_out)[...], frames)
        each_peer(frames, f, lambda o, to, fr: cot_copy(m, o, to, f).start())
        cots[mine(m), f] = cot_slots[m, f]

    def share_copy(m, g):
        piece = cots.at[mine(m), g]
        return remote(piece, piece, es.at[m, g], er.at[m, g], expert=partner)

    def share(m, first, last):
        def step(o, to, fr):
            cot_copy(m, o, to, fr).wait_recv()
            share_copy(m, fr).start()

        each_peer(frames, f, step, first, last)

    def each_frame(fn):
        def step(g, carry):
            fn(g)
            return carry

        lax.fori_loop(0, frames, step, 0)

    small[1].wait()
    send_cot(0)
    small[2].wait()
    expert_ids = lax.broadcasted_iota(jnp.int32, router.shape, 0)
    owned = expert_ids == (f * depth + z) // 2
    column[...] = jnp.sum(jnp.where(owned, router[...].astype(F32), 0.0), axis=0, keepdims=True)
    d_gate[...] = jnp.zeros(d_gate.shape, F32)
    d_up[...] = jnp.zeros(d_up.shape, F32)
    d_down[...] = jnp.zeros(d_down.shape, F32)
    for o in range(1, depth):
        place_copy(o, lax.rem(z + depth - o, depth)).wait_recv()
    for o in range(1, depth):
        choose(lax.rem(z + o, depth))
    for c in own_qkv:
        c.wait()
    each_peer(frames, f, lambda o, to, fr: exchange(lambda c: c.wait_recv(), o, to, fr))
    for i in range(3):
        flat[i] = qkv[i].reshape(tokens, width)
    attend(flat.at[0], flat.at[1], flat.at[2], flat.at[3], acc, positions)
    mix[...] = flat[3].reshape(frames, positions, width)

    def home(o, to, source):
        return remote(mix.at[to], att.at[source], ats.at[o], atr.at[o], frames=to)

    each_peer(frames, f, lambda o, to, fr: home(o, to, f).start())
    att[f] = mix[f]
    cross_copy().wait_recv()
    send_cot(1)
    early = frames // 2
    share_copy(0, f).start()
    share(0, 1, early)
    each_peer(frames, f, lambda o, to, fr: home(o, to, fr).wait_recv())
    for c in [project] + small[3:]:
        c.wait()
    stream = residual[...].astype(F32) + jnp.dot(
        att[...].reshape(tokens, width), proj[...], preferred_element_type=F32
    )
    hid = stream.astype(BF)
    hidden[...] = hid
    hf = hid.astype(F32)
    inv = lax.rsqrt(jnp.mean(hf * hf, axis=-1, keepdims=True) + 1e-06)
    held[z] = (hf * inv * gain[...].reshape(1, width)).astype(BF)

    relay = Relay(depth, z, held, zs, zr)
    relay.start(z)

    def slot_copy(n, o, to, source):
        b = turn(n, z)
        return remote(out_slots.at[b, to], x.at[b, source], xs.at[n, o], xr.at[n, o], frames=to)

    def send_slots(n):
        b = turn(n, z)
        if n:
            relay.arrive(b)
            relay.start(b)
        out_slots[b] = pick_rows(pick[b], held[b], frames)
        each_peer(frames, f, lambda o, to, fr: slot_copy(n, o, to, f).start(), cut if n == 1 else 1)
        x[b, f] = out_slots[b, f]

    def lend_copy(o, g):
        piece = x.at[z, g]
        return remote(piece, piece, hs.at[o], hr.at[o], expert=partner)

    def lend():
        each_peer(frames, f, lambda o, to, fr: lend_copy(o, fr).start(), 1, cut)

    def result_copy(n, i, o, to, source):
        b = turn(n, z)
        return remote(
            yr.at[b, i, to], back.at[b, i, source], ys.at[n, i, o], yr_sem.at[n, i, o], frames=to
        )

    def send_results(n, i):
        b = turn(n, z)
        each_peer(frames, f, lambda o, to, fr: result_copy(n, i, o, to, f).start())
        back[b, i, f] = yr[b, i, f]

    def compute(n):
        b = turn(n, z)
        each_peer(frames, f, lambda o, to, fr: slot_copy(n, o, to, fr).wait_recv(), cut)

        @pl.when(n == 1)
        def _():
            each_frame(lambda g: share_copy(0, g).wait_recv())
            each_peer(frames, f, lambda o, to, fr: lend_copy(o, fr).wait_recv(), 1, cut)

        @pl.when(n != 1)
        def _():
            each_peer(frames, f, lambda o, to, fr: slot_copy(n, o, to, fr).wait_recv(), 1, cut)

        @pl.when((n > 1) & (b != across))
        def _():
            each_frame(lambda g: share_copy(1, g).wait_recv())

        xv = x[b].reshape(slots, width)
        cv = cots[b].reshape(slots, width)
        wr = column[...]
        combine = jax.nn.sigmoid(jnp.sum(xv.astype(F32) * wr, axis=-1, keepdims=True))
        cf = cv.astype(F32)
        scaled = (combine * cf).astype(BF)
        pre_gate = dot(xv, gate[...], 1, 0)
        pre_up = dot(xv, up[...], 1, 0)
        sig = jax.nn.sigmoid(pre_gate)
        act = pre_gate * sig
        units = (act * pre_up).astype(BF)
        out = dot(units, down[...], 1, 0).astype(BF).astype(F32)
        yr[b, 0] = (combine * out).astype(BF).reshape(frames, capacity, width)

        @pl.when(n > 0)
        def _():
            send_results(n, 0)

        d_units = dot(scaled, down[...], 1, 1)
        dpg = (d_units * pre_up * (sig + act * (1.0 - sig))).astype(BF)
        dpu = (d_units * act).astype(BF)
        d_logit = jnp.sum(cf * out, axis=-1, keepdims=True) * combine * (1.0 - combine)
        d_in = dot(dpg, gate[...], 1, 1) + dot(dpu, up[...], 1, 1)
        yr[b, 1] = (d_in + d_logit * wr).astype(BF).reshape(frames, capacity, width)

        @pl.when(n > 0)
        def _():
            send_results(n, 1)

        d_gate[...] += dot(xv, dpg, 0, 0)
        d_up[...] += dot(xv, dpu, 0, 0)
        d_down[...] += dot(units, scaled, 0, 0)

    def totals(n, arrays=(0, 1)):
        b = turn(n, z)
        for i in arrays:
            each_peer(frames, f, lambda o, to, fr: result_copy(n, i, o, to, fr).wait_recv())
            yield dot(pick[b], back[b, i].reshape(slots, width), 0, 0)

    outer = (z == 0) | (z == depth - 1)
    opposite = jnp.where(z == halves, halves - 1, halves)

    def inward(n, i):
        return remote(
            part.at[n, i], passed.at[n - 2, i], psem.at[0, n - 2, i], psem.at[1, n - 2, i], expert=partner
        )

    def over(n, i):
        return remote(
            part.at[n, i], far.at[n - 2, i], fsem.at[0, n - 2, i], fsem.at[1, n - 2, i], expert=opposite
        )

    def near_copy(i):
        return remote(part.at[1, i], near.at[i], nsem.at[0, i], nsem.at[1, i], expert=partner)

    def collect(n, i):
        (total,) = totals(n, (i,))
        part[n, i] = total.astype(BF)

        @pl.when(outer)
        def _():
            inward(n, i).start()

    def forward(n, i):
        @pl.when(jnp.logical_not(outer))
        def _():
            inward(n, i).wait_recv()
            part[n, i] = (part[n, i].astype(F32) + passed[n - 2, i].astype(F32)).astype(BF)
            over(n, i).start()

    def hand_over():
        for i, total in enumerate(totals(1)):

            @pl.when(outer)
            def _():
                part[1, i] = total.astype(BF)

            @pl.when(jnp.logical_not(outer))
            def _():
                over(3, i).wait_recv()
                part[1, i] = (total + far[1, i].astype(F32)).astype(BF)

            near_copy(i).start()

    def share_rest():
        share_copy(1, f).start()
        share(1, 1, frames)
        each_peer(frames, f, lambda o, to, fr: share_copy(0, fr).start(), early)

    send_slots(0)
    each_peer(frames, f, lambda o, to, fr: cot_copy(0, o, to, fr).wait_recv(), early)

    @pl.when(outer)
    def _():
        share_rest()

    for n in range(1, depth - 1):
        send_slots(n)
    for c in loads:
        c.wait()
    compute(0)
    send_slots(depth - 1)

    @pl.when(jnp.logical_not(outer))
    def _():
        share_rest()

    lend()

    def step(i, carry):
        @pl.when(i == depth - 2)
        def _():
            collect(2, 0)
            collect(2, 1)
            forward(2, 0)

        compute(jnp.where(i == depth - 2, 1, i + 2))
        return carry

    lax.fori_loop(0, depth - 1, step, 0)
    for i in range(2):
        send_results(0, i)
    for n in range(depth):
        each_peer(
            frames, f, lambda o, to, fr: slot_copy(n, o, to, f).wait_send(), cut if n == 1 else 1
        )
    each_peer(frames, f, lambda o, to, fr: lend_copy(o, to).wait_send(), 1, cut)
    relay.finish()
    cross_copy().wait_send()
    for o in range(1, depth):
        place_copy(o, z).wait_send()
    for m in range(2):
        each_peer(frames, f, lambda o, to, fr: cot_copy(m, o, to, f).wait_send())
        each_frame(lambda g: share_copy(m, g).wait_send())
    each_peer(frames, f, lambda o, to, fr: exchange(lambda c: c.wait_send(), o, to, f))
    each_peer(frames, f, lambda o, to, fr: home(o, to, f).wait_send())
    forward(2, 1)
    for i in range(2):
        collect(3, i)
        forward(3, i)
    hand_over()
    own = list(totals(0))

    for i in range(2):
        near_copy(i).wait_recv()
        sums[i] = own[i] + near[i].astype(F32)

    @pl.when(jnp.logical_not(outer))
    def _():
        for i in range(2):
            over(2, i).wait_recv()
            sums[i] += far[0, i].astype(F32)

    for i in range(2):
        near_copy(i).wait_send()
        for n in range(2, depth):

            @pl.when(outer)
            def _():
                inward(n, i).wait_send()

            @pl.when(jnp.logical_not(outer))
            def _():
                over(n, i).wait_send()

    for n in range(depth):
        for i in range(2):
            each_peer(frames, f, lambda o, to, fr: result_copy(n, i, o, to, f).wait_send())


def fused(q, k, v, d_out, routes, residual, w_out, gain, router, gate, up, down, depth, capacity):
    frames, positions, width = q.shape
    tokens = frames * positions
    dma = pltpu.SemaphoreType.DMA
    vm = pl.BlockSpec(memory_space=VM)
    hbm = pl.BlockSpec(memory_space=pltpu.HBM)
    slots = (depth, frames, capacity, width)
    pair = (depth, 2, frames, capacity, width)
    blocks = (depth, tokens, width)
    chunked = (frames, positions, width)
    two = (2, tokens, width)
    return pl.pallas_call(
        functools.partial(fused_body, frames, depth),
        in_specs=[hbm] * 12,
        out_specs=[vm] * 5,
        out_shape=[
            VM((tokens, width), BF),
            VM(two, F32),
            VM(gate.shape, F32),
            VM(up.shape, F32),
            VM(down.shape, F32),
        ],
        scratch_shapes=[
            VM(routes.shape, routes.dtype), VM(residual.shape, BF), VM(gain.shape, F32), VM(router.shape, BF),
            VM(w_out.shape, BF), VM((1, width), F32),
            VM((3,) + chunked, BF), VM((4, tokens, width), BF), VM((tokens, width), F32),
            VM(chunked, BF), VM(chunked, BF),
            VM((depth, depth // 2, frames, tokens), F32),
            VM((depth, frames * capacity, tokens), BF),
            VM((tokens, width), BF), VM((tokens, width), BF), VM(blocks, BF),
            VM((2,) + slots[1:], BF), VM(slots, BF), VM(slots, BF), VM(slots, BF),
            VM(gate.shape, BF), VM(up.shape, BF), VM(down.shape, BF),
            VM(pair, BF), VM(pair, BF),
            VM((depth,) + two, BF), VM((2,) + two, BF), VM(two, BF), VM((2,) + two, BF),
            dma((3, frames)), dma((3, frames)), dma((frames,)), dma((frames,)),
            dma((depth,)), dma((depth,)),
            dma((2,)), dma((2, depth)), dma((depth,)),
            dma((2, frames)), dma((2, frames)), dma((2, frames)), dma((2, frames)),
            dma((frames,)), dma((frames,)),
            dma((depth, frames)), dma((depth, frames)),
            dma((depth, 2, frames)), dma((depth, 2, frames)),
            dma((2, 2)), dma((2, 2, 2)), dma((2, 2, 2)), dma((12,)),
        ],
        compiler_params=pltpu.CompilerParams(
            collective_id=0, has_side_effects=True, vmem_limit_bytes=52 * 2**20
        ),
    )(q, k, v, d_out, routes, residual, w_out, gain, router, gate, up, down)


def on_device(
    residual, queries, keys_in, values, w_out, norm_gain, w_router, routes, w_gate, w_up, w_down, d_out
):
    _, tokens, width = residual.shape
    frames, depth = lax.axis_size("frames"), lax.axis_size("expert")
    f, z = lax.axis_index("frames"), lax.axis_index("expert")
    expert_count = w_router.shape[1]
    capacity = 4 * tokens // expert_count
    positions = tokens // frames

    def across(t):
        return lax.all_to_all(
            t.reshape(frames, -1, width), "frames", split_axis=0, concat_axis=0, tiled=True
        )


    own = (f * depth + z) // 2
    router = lax.dynamic_slice(w_router, (0, own), (width, 1)).reshape(1, width)
    if positions % 16 == 0 and capacity % 16 == 0 and depth == 4 and frames & (frames - 1) == 0:
        rows = d_out.reshape(tokens, width)
        hidden, sums, *grads = fused(
            *(t.reshape(frames, positions, width) for t in (queries, keys_in, values)),
            rows, routes.reshape(tokens, 2).T, residual.reshape(tokens, width), w_out, norm_gain,
            w_router.T, w_gate[0], w_up[0], w_down[0], depth, capacity,
        )
        block_out, d_hidden, *grads = tail(hidden, sums, rows, norm_gain, grads)
        return (
            block_out.reshape(residual.shape), d_hidden.reshape(residual.shape),
            *(g[None] for g in grads),
        )

    routes_z = lax.all_gather(routes.reshape(tokens, 2), "expert", axis=0)
    pick = picker(routes_z, expert_count, capacity, frames, depth, z)
    def dispatch(rows):
        gathered = lax.all_gather(rows, "expert", axis=0)
        picked = jnp.einsum("gst,gtd->gsd", pick, gathered, preferred_element_type=F32).astype(BF)
        picked = picked.reshape(depth, frames, capacity, width).transpose(1, 0, 2, 3)
        return across(picked).reshape(frames * depth * capacity, width)

    q, k, v = (across(t).reshape(tokens, width) for t in (queries, keys_in, values))
    cot = dispatch(d_out.reshape(tokens, width))
    attended = across(attention(q, k, v, positions)).reshape(tokens, width)
    stream = residual.reshape(tokens, width).astype(F32) + jnp.dot(
        attended, w_out, preferred_element_type=F32
    )
    hidden = stream.astype(BF)
    hidden_float = hidden.astype(F32)
    inv_rms = lax.rsqrt(jnp.mean(hidden_float * hidden_float, axis=-1, keepdims=True) + 1e-06)
    normed = (hidden_float * inv_rms * norm_gain).astype(BF)
    x = dispatch(normed)
    y, r, d_gate, d_up, d_down = expert(x, cot, router, w_gate[0], w_up[0], w_down[0])

    def collect(rows):
        back = across(rows).reshape(frames, depth, capacity, width).transpose(1, 0, 2, 3)
        back = back.reshape(depth, frames * capacity, width)
        sums = jnp.einsum("gst,gsd->gtd", pick, back, preferred_element_type=F32).astype(BF)
        return lax.psum_scatter(sums, "expert", scatter_dimension=0, tiled=True)[0].astype(F32)

    expert_sum = collect(y)
    d_normed = collect(r)
    return finish(
        residual, d_out, norm_gain, hidden_float, inv_rms, expert_sum, d_normed, d_gate, d_up, d_down
    )


def finish(
    residual, d_out, norm_gain, hidden_float, inv_rms, expert_sum, d_normed, d_gate, d_up, d_down
):
    cotangent = d_out.reshape(hidden_float.shape).astype(F32)
    block_out = (hidden_float + expert_sum).astype(BF).reshape(residual.shape)
    gained = d_normed * norm_gain
    d_norm_in = inv_rms * gained - hidden_float * inv_rms**3 * jnp.mean(
        gained * hidden_float, axis=-1, keepdims=True
    )
    d_hidden = (cotangent + d_norm_in).astype(BF).reshape(residual.shape)
    return (block_out, d_hidden, d_gate[None], d_up[None], d_down[None])


def solution(mesh):
    tok = P("frames", "expert", None)
    both = P(("frames", "expert"), None, None)
    return jax.shard_map(
        on_device,
        mesh=mesh,
        in_specs=(tok, tok, tok, tok, P(), P(), P(), P("expert", "frames", None, None), both, both, both, tok),
        out_specs=(tok, tok, both, both, both),
        check_vma=False,
    )
```
